512 devices in a mesh: layer: 8 (over y, core), latent: 64 (over x, z).
Axes of the slice: x: 4, y: 4, z: 16, core: 2. Of those that a mesh axis runs over, the one named last changes fastest.
Arguments:
- resid: bfloat16 [4, 128, 3584], P(None, 'latent'), may hold values from -6 to 6
- target: bfloat16 [5, 128, 3584], P(None, 'latent'), may hold values from -6 to 6
- enc_weight: bfloat16 [8, 3584, 8192], P('layer', None, 'latent'), may hold values from -0.09375 to 0.09375
- enc_bias: float32 [8, 8192], P('layer', 'latent'), may hold values from -3 to 3
- dec_weight: bfloat16 [8, 2, 2, 8192, 1792], P('layer', None, None, 'latent'), may hold values from -0.046875 to 0.046875
- blocks: int32 [4, 1, 96], replicated, may hold values from 0 to 127, all different within a row
Outputs:
- errors: bfloat16 [8, 128, 1792], P('layer', 'latent')
- enc_grad: bfloat16 [8, 3584, 8192], P('layer', None, 'latent')
- bias_grad: float32 [8, 8192], P('layer', 'latent')
The draws below stay inside these ranges and needn't reach their ends.
Inputs may be any that keep to these rules, and one draw needn't show every extreme that they name: Each row names 96 different blocks; every block is named in some row.
All inputs are finite; a program needn't handle non-finite values.
Results may differ from the reference program's by a relative error of at most 0.007.
Values may be sent and summed in bfloat16 or wider, within the bound.
A program may use at most 64 MiB of HBM per device.

```python
import jax
import jax.numpy as jnp
from jax import lax

D = 3584
DH = 1792
BLOCK = 128
LATENTS = 16384
HALF = 8192
BLOCKS = 128
ACTIVE = 96
LAYERS = 4
TOKENS = 128
TILE = 128


def levels(own_key, extent, pieces, low, high):
    factor_of = 1.0
    for position, shards_of in pieces:
        heights = jax.random.uniform(jax.random.fold_in(jax.random.fold_in(own_key, 6), position), (shards_of,), jnp.float32, low / len(pieces), high / len(pieces))
        factor_of = factor_of * jnp.repeat(jnp.exp(heights), extent[position] // shards_of).reshape((-1,) + (1,) * (len(extent) - 1 - position))
    return factor_of


def picks_of(rng, rows, number_of, top, lift):
    ranking = jax.random.permutation(jax.random.fold_in(rng, 1), number_of)
    favour = ranking
    for power in range(3):
        favour = favour * favour // number_of
    favour = favour * lift // number_of
    tickets = jax.random.randint(jax.random.fold_in(rng, 2), (rows, number_of), 0, 4096) + favour
    sure = jax.random.permutation(jax.random.fold_in(rng, 3), rows)[jnp.arange(number_of) % rows]
    tickets = jnp.where(jnp.arange(rows)[:, None] == sure[None, :], 1 << 14, tickets)
    merit = tickets * number_of + jnp.arange(number_of)
    return lax.top_k(merit.astype(jnp.int32), top)[1].astype(jnp.int32)


def gaussian(stream_key, dims, deviation, limit, pieces=(), kind=jnp.bfloat16):
    array = deviation * jax.random.normal(stream_key, dims, jnp.float32)
    if pieces:
        array = array * levels(stream_key, dims, pieces, -0.22, 0.18)
    return jnp.clip(array, -limit, limit).astype(kind)


def setup_inputs(seed: int = 0) -> dict:
    seeds = jax.random.split(jax.random.key(seed), 7)
    resid = gaussian(seeds[0], (LAYERS, TOKENS, D), 1.0, 6.0, ((1, 64),))
    target = gaussian(seeds[1], (LAYERS + 1, TOKENS, D), 1.0, 6.0, ((1, 64),))
    enc_weight = gaussian(seeds[2], (2 * LAYERS, D, HALF), D ** -0.5, 0.09375, ((0, 8), (2, 64)))
    enc_bias = gaussian(seeds[3], (2 * LAYERS, HALF), 0.5, 3.0, ((0, 8), (1, 64)), jnp.float32)
    dec_weight = gaussian(seeds[4], (2 * LAYERS, 2, 2, HALF, DH), LATENTS ** -0.5, 0.046875, ((0, 8), (3, 64)))
    blocks = picks_of(seeds[5], LAYERS * (TOKENS // TILE), BLOCKS, ACTIVE, 12000).reshape((LAYERS, TOKENS // TILE, ACTIVE))
    return {"resid": resid, "target": target, "enc_weight": enc_weight, "enc_bias": enc_bias, "dec_weight": dec_weight, "blocks": blocks}


def decoder_of(dec_weight, layer_pos, target_pos):
    left_cols = dec_weight[2 * layer_pos, target_pos].reshape(LATENTS, DH)
    right_cols = dec_weight[2 * layer_pos + 1, target_pos].reshape(LATENTS, DH)
    return jnp.concatenate([left_cols, right_cols], axis=1)


def reference(resid, target, enc_weight, enc_bias, dec_weight, blocks):
    block_ids = jnp.arange(LATENTS, dtype=jnp.int32) // BLOCK
    activations = []
    gate_masks = []
    for index in range(LAYERS):
        encoder = jnp.concatenate([enc_weight[2 * index], enc_weight[2 * index + 1]], axis=1)
        bias_row = jnp.concatenate([enc_bias[2 * index], enc_bias[2 * index + 1]])
        preact = jnp.dot(resid[index], encoder, preferred_element_type=jnp.float32) + bias_row
        listed = jnp.any(blocks[index][:, :, None] == block_ids[None, None, :], axis=1)
        gate_mask = jnp.repeat(listed.astype(jnp.float32), TILE, axis=0)
        activations.append((preact * gate_mask).astype(jnp.bfloat16))
        gate_masks.append(gate_mask)
    recon = [jnp.zeros((TOKENS, D), jnp.float32) for index in range(LAYERS + 1)]
    for index in range(LAYERS):
        for step in range(2):
            recon[index + step] = recon[index + step] + jnp.dot(activations[index], decoder_of(dec_weight, index, step), preferred_element_type=jnp.float32)
    error_list = [(recon[index] - target[index].astype(jnp.float32)).astype(jnp.bfloat16) for index in range(LAYERS + 1)]
    error_rows = []
    grad_rows = []
    bias_rows = []
    for index in range(LAYERS):
        grad_act = jnp.dot(error_list[index], decoder_of(dec_weight, index, 0).T, preferred_element_type=jnp.float32)
        grad_act = grad_act + jnp.dot(error_list[index + 1], decoder_of(dec_weight, index, 1).T, preferred_element_type=jnp.float32)
        grad_pre = grad_act * gate_masks[index]
        bias_full = jnp.sum(grad_pre, axis=0)
        grad_full = jnp.dot(resid[index].T, grad_pre.astype(jnp.bfloat16), preferred_element_type=jnp.float32).astype(jnp.bfloat16)
        for which_half in range(2):
            error_rows.append(error_list[index][:, which_half * DH:(which_half + 1) * DH])
            grad_rows.append(grad_full[:, which_half * HALF:(which_half + 1) * HALF])
            bias_rows.append(bias_full[which_half * HALF:(which_half + 1) * HALF])
    return jnp.stack(error_rows), jnp.stack(grad_rows), jnp.stack(bias_rows)
```

```python
import functools

import jax
import jax.numpy as jnp
from jax import lax
from jax.experimental import pallas as pl
from jax.experimental.pallas import tpu as pltpu
from jax.sharding import Mesh
from jax.sharding import PartitionSpec as P

NY, NX, NZ = 4, 4, 16
NA = 4
F32, BF16 = jnp.float32, jnp.bfloat16
SENDS = 160
FAR_GREETING = True


def body(
    resid, target, enc, bias, dec, blocks,
    x_out, low_out, bias_out, err_out,
    X, XO, XS, WE, BI, DW, TG, PP, PR, S0, S1, R0, R1, B0, B1, Q0, Q1,
    S2, S2F, R2, YO, YA, YN, YB, E, EM, GP, GR, loc, ssem, rsem,
):
    y, h = lax.axis_index("y"), lax.axis_index("core")
    x, z = lax.axis_index("x"), lax.axis_index("z")
    other = 1 - h
    r, a = lax.rem(z, 4), lax.div(z, 4)
    half = XO.shape[-1]
    width = bias.shape[-1]

    def at_x(d):
        return {"x": lax.rem(x + d, NX)}

    def at_z(d):
        return {"z": lax.rem(z + d + NZ, NZ)}

    sibling = {"core": other}

    barrier = pltpu.get_barrier_semaphore()
    near = [sibling, at_x(1), at_x(2), at_x(3), at_z(1), at_z(-1)]
    if FAR_GREETING:
        near += [at_z(d) for d in (2, -2, 4, -4, 8)]
    for peer in near:
        pl.semaphore_signal(barrier, inc=1, device_id=peer, device_id_type=pl.DeviceIdType.MESH)

    @pl.when(y > 0)
    def _():
        pl.semaphore_signal(barrier, inc=1, device_id={"y": y - 1}, device_id_type=pl.DeviceIdType.MESH)

    @pl.when(y < NY - 1)
    def _():
        pl.semaphore_signal(barrier, inc=1, device_id={"y": y + 1}, device_id_type=pl.DeviceIdType.MESH)

    mine = resid.at[y, :, pl.ds(pl.multiple_of(h * half, 128), half)]
    keep = pltpu.make_async_copy(mine, X.at[r, x, a], loc.at[0])
    keep.start()
    enc_own = pltpu.make_async_copy(
        enc.at[0, pl.ds(pl.multiple_of(h * half, 128), half), :],
        WE.at[:, pl.ds(pl.multiple_of(h * width, 128), width)], loc.at[1])
    enc_own.start()
    bias_own = pltpu.make_async_copy(bias, BI.at[h], loc.at[2])
    bias_own.start()
    tgt = pltpu.make_async_copy(
        target.at[pl.ds(y, 2), :, pl.ds(pl.multiple_of(h * half, 128), half)], TG, loc.at[3])
    tgt.start()
    dec_in = pltpu.make_async_copy(dec.at[0], DW, loc.at[4])
    dec_in.start()

    extra = jnp.where(jnp.logical_and(y > 0, y < NY - 1), 2, 1)
    pl.semaphore_wait(barrier, len(near) + extra)

    count = [0]
    started = []

    def made(src, dst, peer):
        k = count[0]
        count[0] += 1
        return pltpu.make_async_remote_copy(
            src_ref=src, dst_ref=dst, send_sem=ssem.at[k], recv_sem=rsem.at[k],
            device_id=peer, device_id_type=pl.DeviceIdType.MESH)

    def send(src, dst, peer):
        copy = made(src, dst, peer)
        copy.start()
        started.append(copy)
        return copy

    def slot(d):
        zz = lax.rem(z + d + NZ, NZ)
        return lax.rem(zz, 4), lax.div(zz, 4)

    up = send(mine, X.at[r, x, a], at_z(1))
    down = send(mine, X.at[r, x, a], at_z(-1))
    across = [send(mine, X.at[r, x, a], at_x(d)) for d in (2, 1, 3)]
    enc_far = send(
        enc.at[0, pl.ds(pl.multiple_of(other * half, 128), half), :],
        WE.at[:, pl.ds(pl.multiple_of(h * width, 128), width)], sibling)
    bias_far = send(bias, BI.at[h], sibling)
    for s in range(1, 9):
        up.wait_recv()
        rr, aa = slot(-s)
        got = X.at[rr, x, aa]
        if s < 8:
            up = send(got, got, at_z(1))
        across += [send(got, got, at_x(d)) for d in (2, 1, 3)]
        if s < 8:
            down.wait_recv()
            rr, aa = slot(s)
            got = X.at[rr, x, aa]
            if s < 7:
                down = send(got, got, at_z(-1))
            across += [send(got, got, at_x(d)) for d in (2, 1, 3)]

    row = blocks[y]
    column = x * NZ + z
    hits = [
        jnp.max((row == g * NX * NZ + column).astype(F32), axis=1, keepdims=True)
        for g in range(2)
    ]
    lanes = lax.broadcasted_iota(jnp.int32, (1, 2 * width), 1)
    gates = jnp.where(lanes < width, hits[0], hits[1])
    gate_own = jnp.where(h == 0, hits[0], hits[1])

    bias_far.wait_recv()
    bias_own.wait()
    enc_far.wait_recv()
    enc_own.wait()
    keep.wait()
    for copy in across:
        copy.wait_recv()
    rows = 4 * NX * NA * 2
    for rr in range(4):
        XO[pl.ds(rr * 32, 32), :] = X[rr].reshape(32, half)
    PP[...] = jnp.dot(XO[...], WE[...], preferred_element_type=F32)
    part = send(PP, PR, sibling)
    rows_far = send(XO, XS, sibling)
    part.wait_recv()
    biases = jnp.concatenate([BI[0], BI[1]], axis=1)
    acts = ((PP[...] + PR[...] + biases) * gates).astype(BF16)

    dec_in.wait()
    step = 256
    for t, S in ((1, S1), (0, S0)):
        for n in range(0, half, step):
            w = DW[t, :, :, n:n + step].reshape(2 * width, step)
            p = jnp.dot(acts, w, preferred_element_type=F32)
            S[:, :, :, n:n + step] = p.reshape(4, NX, 8, step).astype(BF16)
        if t == 1:
            r1, r3, r2 = lax.rem(r + 1, 4), lax.rem(r + 3, 4), lax.rem(r + 2, 4)
            in1 = [
                send(S1.at[r2, pl.ds(0, 2)], R1.at[2, pl.ds(0, 2)], at_z(2)),
                send(S1.at[r2, pl.ds(2, 2)], R1.at[2, pl.ds(2, 2)], at_z(-2)),
                send(S1.at[r1], R1.at[0], at_z(1)),
                send(S1.at[r3], R1.at[1], at_z(-1)),
            ]
        else:
            in0 = [
                send(S0.at[:, lax.rem(x + d, NX)], R0.at[i], at_x(d))
                for i, d in enumerate((2, 1, 3))
            ]
    for copy in in1:
        copy.wait_recv()

    def summed1(xx):
        return (S1[r, xx].astype(F32) + R1[0, xx].astype(F32)) + (
            R1[1, xx].astype(F32) + R1[2, xx].astype(F32))

    def summed0(rr):
        return (S0[rr, x].astype(F32) + R0[0, rr].astype(F32)) + (
            R0[1, rr].astype(F32) + R0[2, rr].astype(F32))

    next1 = []
    for i, d in enumerate((2, 1, 3)):
        B1[i] = summed1(lax.rem(x + d, NX)).astype(BF16)
        next1.append(send(B1.at[i], Q1.at[i], at_x(d)))
    for copy in in0:
        copy.wait_recv()
    next0 = []
    n2 = half // 2
    B0[2] = summed0(r2).astype(BF16)
    next0.append(send(B0.at[2, :, pl.ds(0, n2)], Q0.at[2, :, pl.ds(0, n2)], at_z(2)))
    next0.append(send(B0.at[2, :, pl.ds(n2, n2)], Q0.at[2, :, pl.ds(n2, n2)], at_z(-2)))
    B0[0] = summed0(r1).astype(BF16)
    next0.append(send(B0.at[0], Q0.at[0], at_z(1)))
    B0[1] = summed0(r3).astype(BF16)
    next0.append(send(B0.at[1], Q0.at[1], at_z(-1)))
    own1 = summed1(x)
    own0 = summed0(r)
    for copy in next1 + next0:
        copy.wait_recv()
    for t, own, Q in ((0, own0, Q0), (1, own1, Q1)):
        total = (own + Q[0].astype(F32)) + (Q[1].astype(F32) + Q[2].astype(F32))
        for aa in range(NA):
            two = total[2 * aa:2 * aa + 2, :]
            S2F[aa, t] = two
            S2[aa, t] = two.astype(BF16)
    last = [
        send(S2.at[lax.rem(a + d, NA)], R2.at[i], at_z(4 * d if d < 3 else -4))
        for i, d in enumerate((2, 1, 3))
    ]
    for copy in last:
        copy.wait_recv()
    sums = S2F[a] + R2[0].astype(F32) + R2[1].astype(F32) + R2[2].astype(F32)
    YO[...] = sums[0]
    YA[...] = sums[1]

    up_y = made(YA, YB, {"y": lax.rem(y + 1, NY)})
    down_y = made(YO, YN, {"y": lax.rem(y + NY - 1, NY)})

    @pl.when(y < NY - 1)
    def _():
        up_y.start()

    @pl.when(y > 0)
    def _():
        down_y.start()
        up_y.wait_recv()

    @pl.when(y == 0)
    def _():
        YB[...] = jnp.zeros_like(YB)

    @pl.when(y < NY - 1)
    def _():
        down_y.wait_recv()

    @pl.when(y == NY - 1)
    def _():
        YN[...] = jnp.zeros_like(YN)

    tgt.wait()
    err_own = (sums[0] + YB[...] - TG[0].astype(F32)).astype(BF16)
    err_next = (YN[...] + sums[1] - TG[1].astype(F32)).astype(BF16)
    err_out[0] = err_own
    E[0, r, x, a] = err_own
    E[1, r, x, a] = err_next

    piece = E.at[:, r, x, a]
    gathered = [send(piece, piece, at_z(d)) for d in (8, 4, -4)]
    for copy in gathered:
        copy.wait_recv()
    h2 = NA // 2

    def along_x(t, rr):
        block = E.at[t, rr, x]
        return [send(block, block, at_x(d)) for d in (2, 1, 3)]

    def along_z(t, xx):
        lo, hi = E.at[t, r, xx, pl.ds(0, h2)], E.at[t, r, xx, pl.ds(h2, h2)]
        block = E.at[t, r, xx]
        return [
            send(lo, lo, at_z(-2)), send(hi, hi, at_z(2)),
            send(block, block, at_z(-1)), send(block, block, at_z(1)),
        ]

    first0 = along_z(0, x)
    first1 = along_x(1, r)
    rest = along_x(0, r) + along_z(1, x)
    for d, copy in zip((2, 1, 3), first1):
        copy.wait_recv()
        rest += along_z(1, lax.rem(x + NX - d, NX))
    first0[2].wait_recv()
    rest += along_x(0, r1)
    first0[3].wait_recv()
    rest += along_x(0, r3)
    first0[0].wait_recv()
    first0[1].wait_recv()
    rest += along_x(0, r2)
    for copy in rest:
        copy.wait_recv()
    grad = None
    for t in range(2):
        for rr in range(4):
            EM[pl.ds(rr * 32, 32), :] = E[t, rr].reshape(32, half)
        term = lax.dot_general(
            EM[...], DW[t].reshape(2 * width, half), (((1,), (1,)), ((), ())),
            preferred_element_type=F32)
        grad = term if grad is None else grad + term
    GP[0] = grad[:, :width]
    GP[1] = grad[:, width:]
    back = send(GP.at[other], GR, sibling)

    rows_far.wait_recv()
    out_a = pltpu.make_async_copy(XO, x_out.at[h], loc.at[5])
    out_b = pltpu.make_async_copy(XS, x_out.at[other], loc.at[6])
    out_a.start()
    out_b.start()
    back.wait_recv()
    grad_pre = (GP[h] + GR[...]) * gate_own
    bias_out[...] = jnp.sum(grad_pre, axis=0, keepdims=True)
    low_out[...] = grad_pre.astype(BF16)
    for copy in started:
        copy.wait_send()

    @pl.when(y < NY - 1)
    def _():
        up_y.wait_send()

    @pl.when(y > 0)
    def _():
        down_y.wait_send()

    out_a.wait()
    out_b.wait()


def on_device(resid, target, enc, bias, dec, blocks):
    half = dec.shape[-1]
    width = enc.shape[-1]
    rows = 128
    any_spec = pl.BlockSpec(memory_space=pl.ANY)
    vmem = pl.BlockSpec(memory_space=pltpu.VMEM)
    V = pltpu.VMEM
    x_all, low, bias_grad, errors = pl.pallas_call(
        body,
        out_shape=(
            jax.ShapeDtypeStruct((2, rows, half), BF16),
            jax.ShapeDtypeStruct((rows, width), BF16),
            jax.ShapeDtypeStruct((1, width), F32),
            jax.ShapeDtypeStruct((1, 2, half), BF16),
        ),
        in_specs=[any_spec] * 5 + [vmem],
        out_specs=(any_spec, vmem, vmem, vmem),
        scratch_shapes=[
            V((4, NX, NA, 2, half), BF16),
            V((rows, half), BF16),
            V((rows, half), BF16),
            V((half, 2 * width), BF16),
            V((2, 1, width), F32),
            V((2, 2, width, half), BF16),
            V((2, 2, half), BF16),
            V((rows, 2 * width), F32),
            V((rows, 2 * width), F32),
            V((4, NX, 8, half), BF16),
            V((4, NX, 8, half), BF16),
            V((3, 4, 8, half), BF16),
            V((3, NX, 8, half), BF16),
            V((3, 8, half), BF16),
            V((3, 8, half), BF16),
            V((3, 8, half), BF16),
            V((3, 8, half), BF16),
            V((NA, 2, 2, half), BF16),
            V((NA, 2, 2, half), F32),
            V((3, 2, 2, half), BF16),
            V((2, half), F32),
            V((2, half), F32),
            V((2, half), F32),
            V((2, half), F32),
            V((2, 4, NX, NA, 2, half), BF16),
            V((rows, half), BF16),
            V((2, rows, width), F32),
            V((rows, width), F32),
            pltpu.SemaphoreType.DMA((8,)),
            pltpu.SemaphoreType.DMA((SENDS,)),
            pltpu.SemaphoreType.DMA((SENDS,)),
        ],
        compiler_params=pltpu.CompilerParams(collective_id=0, has_side_effects=True),
        name="step",
    )(resid, target, enc, bias, dec, blocks)
    grad = lax.dot_general(
        x_all, low, (((1,), (0,)), ((), ())), preferred_element_type=F32)
    return errors, grad.astype(BF16).reshape(1, 2 * half, width), bias_grad


def solution(mesh):
    fine = Mesh(mesh.devices.reshape(NY, 2, NX, NZ), ("y", "core", "x", "z"))
    layer, latent = ("y", "core"), ("x", "z")
    return jax.shard_map(
        on_device,
        mesh=fine,
        in_specs=(
            P(None, latent, None), P(None, latent, None), P(layer, None, latent),
            P(layer, latent), P(layer, None, None, latent, None), P(),
        ),
        out_specs=(P(layer, latent, None), P(layer, None, latent), P(layer, latent)),
        check_vma=False,
    )
```

```python
import functools

import jax
import jax.numpy as jnp
from jax import lax
from jax.experimental import pallas as pl
from jax.experimental.pallas import tpu as pltpu
from jax.sharding import Mesh
from jax.sharding import PartitionSpec as P

NY, NX, NZ = 4, 4, 16
NA = 4
F32, BF16 = jnp.float32, jnp.bfloat16
SENDS = 160


def body(
    resid, target, enc, bias, dec, blocks,
    x_out, low_out, bias_out, err_out,
    X, XO, XO_T, XS_T, WE, BI, DW, TG, PP, PR, S0, S1, R0, R1, B0, B1, Q0, Q1,
    S2, S2F, R2, YO, YA, YN, YB, E, EM, GP, GR, loc, ssem, rsem,
):
    y, h = lax.axis_index("y"), lax.axis_index("core")
    x, z = lax.axis_index("x"), lax.axis_index("z")
    other = 1 - h
    r, a = lax.rem(z, 4), lax.div(z, 4)
    half = XO.shape[-1]
    width = bias.shape[-1]

    def at_x(d):
        return {"x": lax.rem(x + d, NX)}

    def at_z(d):
        return {"z": lax.rem(z + d + NZ, NZ)}

    sibling = {"core": other}

    barrier = pltpu.get_barrier_semaphore()
    near = [sibling, at_x(1), at_x(2), at_x(3)]
    near += [at_z(d) for d in (1, -1, 2, -2, 3, -3, 4, -4)]
    for peer in near:
        pl.semaphore_signal(barrier, inc=1, device_id=peer, device_id_type=pl.DeviceIdType.MESH)

    @pl.when(y > 0)
    def _():
        pl.semaphore_signal(barrier, inc=1, device_id={"y": y - 1}, device_id_type=pl.DeviceIdType.MESH)

    @pl.when(y < NY - 1)
    def _():
        pl.semaphore_signal(barrier, inc=1, device_id={"y": y + 1}, device_id_type=pl.DeviceIdType.MESH)

    mine = resid.at[y, :, pl.ds(pl.multiple_of(h * half, 128), half)]
    keep = pltpu.make_async_copy(mine, X.at[r, x, a], loc.at[0])
    keep.start()
    enc_own = pltpu.make_async_copy(
        enc.at[0, pl.ds(pl.multiple_of(h * half, 128), half), :],
        WE.at[:, pl.ds(pl.multiple_of(h * width, 128), width)], loc.at[1])
    enc_own.start()
    bias_own = pltpu.make_async_copy(bias, BI.at[h], loc.at[2])
    bias_own.start()
    tgt = pltpu.make_async_copy(
        target.at[pl.ds(y, 2), :, pl.ds(pl.multiple_of(h * half, 128), half)], TG, loc.at[3])
    tgt.start()
    dec_in = pltpu.make_async_copy(dec.at[0], DW, loc.at[4])
    dec_in.start()

    extra = jnp.where(jnp.logical_and(y > 0, y < NY - 1), 2, 1)
    pl.semaphore_wait(barrier, len(near) + extra)

    count = [0]
    started = []

    def made(src, dst, peer):
        k = count[0]
        count[0] += 1
        return pltpu.make_async_remote_copy(
            src_ref=src, dst_ref=dst, send_sem=ssem.at[k], recv_sem=rsem.at[k],
            device_id=peer, device_id_type=pl.DeviceIdType.MESH)

    def send(src, dst, peer):
        copy = made(src, dst, peer)
        copy.start()
        started.append(copy)
        return copy

    def slot(d):
        zz = lax.rem(z + d + NZ, NZ)
        return lax.rem(zz, 4), lax.div(zz, 4)

    def gathered(buf, src):
        own = buf.at[r, x, a]
        out = {d: send(src, own, at_z(d)) for d in (4, -4, 3, -3, 2, -2, 1, -1)}
        across = [send(src, own, at_x(d)) for d in (2, 1, 3)]

        def passed(d):
            rr, aa = slot(-d)
            got = buf.at[rr, x, aa]
            return got, [send(got, got, at_x(dx)) for dx in (2, 1, 3)]

        for d in (1, -1, 2, -2, 3, -3):
            out[d].wait_recv()
            across += passed(d)[1]
        far = {}
        for d, steps in ((4, (4, 3, 2, 1)), (-4, (-3, -2, -1))):
            out[d].wait_recv()
            rr, aa = slot(-d)
            got = buf.at[rr, x, aa]
            for k in steps:
                far[k + d] = send(got, got, at_z(k))
        for d in (4, -4):
            across += passed(d)[1]
        for d in (5, -5, 6, -6, 7, -7, 8):
            far[d].wait_recv()
            across += passed(d)[1]
        return across

    enc_far = send(
        enc.at[0, pl.ds(pl.multiple_of(other * half, 128), half), :],
        WE.at[:, pl.ds(pl.multiple_of(h * width, 128), width)], sibling)
    bias_far = send(bias, BI.at[h], sibling)
    across = gathered(X, mine)

    row = blocks[y]
    column = x * NZ + z
    hits = [
        jnp.max((row == g * NX * NZ + column).astype(F32), axis=1, keepdims=True)
        for g in range(2)
    ]
    lanes = lax.broadcasted_iota(jnp.int32, (1, 2 * width), 1)
    gates = jnp.where(lanes < width, hits[0], hits[1])
    gate_own = jnp.where(h == 0, hits[0], hits[1])

    bias_far.wait_recv()
    bias_own.wait()
    enc_far.wait_recv()
    enc_own.wait()
    keep.wait()
    for copy in across:
        copy.wait_recv()
    for rr in range(4):
        XO[pl.ds(rr * 32, 32), :] = X[rr].reshape(32, half)
    PP[...] = jnp.dot(XO[...], WE[...], preferred_element_type=F32)
    part = send(PP, PR, sibling)
    part.wait_recv()
    biases = jnp.concatenate([BI[0], BI[1]], axis=1)
    acts = ((PP[...] + PR[...] + biases) * gates).astype(BF16)

    dec_in.wait()
    step = 256
    for t, S in ((1, S1), (0, S0)):
        for n in range(0, half, step):
            w = DW[t, :, :, n:n + step].reshape(2 * width, step)
            p = jnp.dot(acts, w, preferred_element_type=F32)
            S[:, :, :, n:n + step] = p.reshape(4, NX, 8, step).astype(BF16)
        if t == 1:
            r1, r3, r2 = lax.rem(r + 1, 4), lax.rem(r + 3, 4), lax.rem(r + 2, 4)
            in1 = [
                send(S1.at[r2, pl.ds(0, 2)], R1.at[2, pl.ds(0, 2)], at_z(2)),
                send(S1.at[r2, pl.ds(2, 2)], R1.at[2, pl.ds(2, 2)], at_z(-2)),
                send(S1.at[r1], R1.at[0], at_z(1)),
                send(S1.at[r3], R1.at[1], at_z(-1)),
            ]
        else:
            in0 = [
                send(S0.at[:, lax.rem(x + d, NX)], R0.at[i], at_x(d))
                for i, d in enumerate((2, 1, 3))
            ]
    for n in range(0, half, step):
        XO_T[n:n + step, :] = XO[:, n:n + step].T
    rows_far = send(XO_T, XS_T, sibling)
    for copy in in1:
        copy.wait_recv()

    def summed1(xx):
        return (S1[r, xx].astype(F32) + R1[0, xx].astype(F32)) + (
            R1[1, xx].astype(F32) + R1[2, xx].astype(F32))

    def summed0(rr):
        return (S0[rr, x].astype(F32) + R0[0, rr].astype(F32)) + (
            R0[1, rr].astype(F32) + R0[2, rr].astype(F32))

    next1 = []
    for i, d in enumerate((2, 1, 3)):
        B1[i] = summed1(lax.rem(x + d, NX)).astype(BF16)
        next1.append(send(B1.at[i], Q1.at[i], at_x(d)))
    for copy in in0:
        copy.wait_recv()
    next0 = []
    n2 = half // 2
    B0[2] = summed0(r2).astype(BF16)
    next0.append(send(B0.at[2, :, pl.ds(0, n2)], Q0.at[2, :, pl.ds(0, n2)], at_z(2)))
    next0.append(send(B0.at[2, :, pl.ds(n2, n2)], Q0.at[2, :, pl.ds(n2, n2)], at_z(-2)))
    B0[0] = summed0(r1).astype(BF16)
    next0.append(send(B0.at[0], Q0.at[0], at_z(1)))
    B0[1] = summed0(r3).astype(BF16)
    next0.append(send(B0.at[1], Q0.at[1], at_z(-1)))
    own1 = summed1(x)
    own0 = summed0(r)
    for copy in next1 + next0:
        copy.wait_recv()
    for t, own, Q in ((0, own0, Q0), (1, own1, Q1)):
        total = (own + Q[0].astype(F32)) + (Q[1].astype(F32) + Q[2].astype(F32))
        for aa in range(NA):
            two = total[2 * aa:2 * aa + 2, :]
            S2F[aa, t] = two
            S2[aa, t] = two.astype(BF16)
    last = [
        send(S2.at[lax.rem(a + d, NA)], R2.at[i], at_z(4 * d if d < 3 else -4))
        for i, d in enumerate((2, 1, 3))
    ]
    for copy in last:
        copy.wait_recv()
    sums = S2F[a] + R2[0].astype(F32) + R2[1].astype(F32) + R2[2].astype(F32)
    YO[...] = sums[0]
    YA[...] = sums[1]

    up_y = made(YA, YB, {"y": lax.rem(y + 1, NY)})
    down_y = made(YO, YN, {"y": lax.rem(y + NY - 1, NY)})

    @pl.when(y < NY - 1)
    def _():
        up_y.start()

    @pl.when(y > 0)
    def _():
        down_y.start()
        up_y.wait_recv()

    @pl.when(y == 0)
    def _():
        YB[...] = jnp.zeros_like(YB)

    @pl.when(y < NY - 1)
    def _():
        down_y.wait_recv()

    @pl.when(y == NY - 1)
    def _():
        YN[...] = jnp.zeros_like(YN)

    tgt.wait()
    err_own = (sums[0] + YB[...] - TG[0].astype(F32)).astype(BF16)
    err_next = (YN[...] + sums[1] - TG[1].astype(F32)).astype(BF16)
    err_out[0] = err_own
    E[r, x, a, 0] = err_own
    E[r, x, a, 1] = err_next

    rows_far.wait_recv()
    out_a = pltpu.make_async_copy(XO_T, x_out.at[h], loc.at[5])
    out_b = pltpu.make_async_copy(XS_T, x_out.at[other], loc.at[6])
    out_a.start()
    out_b.start()

    for copy in gathered(E, E.at[r, x, a]):
        copy.wait_recv()
    grad = None
    for t in range(2):
        for rr in range(4):
            EM[pl.ds(rr * 32, 32), :] = E[rr, :, :, t].reshape(32, half)
        term = lax.dot_general(
            EM[...], DW[t].reshape(2 * width, half), (((1,), (1,)), ((), ())),
            preferred_element_type=F32)
        grad = term if grad is None else grad + term
    GP[0] = grad[:, :width]
    GP[1] = grad[:, width:]
    back = send(GP.at[other], GR, sibling)

    back.wait_recv()
    grad_pre = (GP[h] + GR[...]) * gate_own
    bias_out[...] = jnp.sum(grad_pre, axis=0, keepdims=True)
    low_out[...] = grad_pre.astype(BF16)
    for copy in started:
        copy.wait_send()

    @pl.when(y < NY - 1)
    def _():
        up_y.wait_send()

    @pl.when(y > 0)
    def _():
        down_y.wait_send()

    out_a.wait()
    out_b.wait()


def on_device(resid, target, enc, bias, dec, blocks):
    half = dec.shape[-1]
    width = enc.shape[-1]
    rows = 128
    any_spec = pl.BlockSpec(memory_space=pl.ANY)
    vmem = pl.BlockSpec(memory_space=pltpu.VMEM)
    V = pltpu.VMEM
    x_all, low, bias_grad, errors = pl.pallas_call(
        body,
        out_shape=(
            jax.ShapeDtypeStruct((2, half, rows), BF16),
            jax.ShapeDtypeStruct((rows, width), BF16),
            jax.ShapeDtypeStruct((1, width), F32),
            jax.ShapeDtypeStruct((1, 2, half), BF16),
        ),
        in_specs=[any_spec] * 5 + [vmem],
        out_specs=(any_spec, vmem, vmem, vmem),
        scratch_shapes=[
            V((4, NX, NA, 2, half), BF16),
            V((rows, half), BF16),
            V((half, rows), BF16),
            V((half, rows), BF16),
            V((half, 2 * width), BF16),
            V((2, 1, width), F32),
            V((2, 2, width, half), BF16),
            V((2, 2, half), BF16),
            V((rows, 2 * width), F32),
            V((rows, 2 * width), F32),
            V((4, NX, 8, half), BF16),
            V((4, NX, 8, half), BF16),
            V((3, 4, 8, half), BF16),
            V((3, NX, 8, half), BF16),
            V((3, 8, half), BF16),
            V((3, 8, half), BF16),
            V((3, 8, half), BF16),
            V((3, 8, half), BF16),
            V((NA, 2, 2, half), BF16),
            V((NA, 2, 2, half), F32),
            V((3, 2, 2, half), BF16),
            V((2, half), F32),
            V((2, half), F32),
            V((2, half), F32),
            V((2, half), F32),
            V((4, NX, NA, 2, 2, half), BF16),
            V((rows, half), BF16),
            V((2, rows, width), F32),
            V((rows, width), F32),
            pltpu.SemaphoreType.DMA((8,)),
            pltpu.SemaphoreType.DMA((SENDS,)),
            pltpu.SemaphoreType.DMA((SENDS,)),
        ],
        compiler_params=pltpu.CompilerParams(collective_id=0, has_side_effects=True),
        name="step",
    )(resid, target, enc, bias, dec, blocks)
    parts = 4
    tall = 2 * half // parts
    grad, bias_grad, errors = pl.pallas_call(
        weight_gradient,
        grid=(parts,),
        out_shape=(
            jax.ShapeDtypeStruct((1, 2 * half, width), BF16),
            jax.ShapeDtypeStruct((1, width), F32),
            jax.ShapeDtypeStruct((1, 2, half), BF16),
        ),
        in_specs=[
            pl.BlockSpec((tall, rows), lambda i: (i, 0)),
            pl.BlockSpec((rows, width), lambda i: (0, 0)),
            pl.BlockSpec((1, width), lambda i: (0, 0)),
            pl.BlockSpec((1, 2, half), lambda i: (0, 0, 0)),
        ],
        out_specs=(
            pl.BlockSpec((1, tall, width), lambda i: (0, i, 0)),
            pl.BlockSpec((1, width), lambda i: (0, 0)),
            pl.BlockSpec((1, 2, half), lambda i: (0, 0, 0)),
        ),
        name="weights",
    )(x_all.reshape(2 * half, rows), low, bias_grad, errors)
    return errors, grad, bias_grad


def weight_gradient(xt, low, bias_in, err_in, grad, bias_out, err_out):
    grad[0] = jnp.dot(xt[...], low[...], preferred_element_type=F32).astype(BF16)

    @pl.when(pl.program_id(0) == 0)
    def _():
        bias_out[...] = bias_in[...]
        err_out[...] = err_in[...]


def solution(mesh):
    fine = Mesh(mesh.devices.reshape(NY, 2, NX, NZ), ("y", "core", "x", "z"))
    layer, latent = ("y", "core"), ("x", "z")
    return jax.shard_map(
        on_device,
        mesh=fine,
        in_specs=(
            P(None, latent, None), P(None, latent, None), P(layer, None, latent),
            P(layer, latent), P(layer, None, None, latent, None), P(),
        ),
        out_specs=(P(layer, latent, None), P(layer, None, latent), P(layer, latent)),
        check_vma=False,
    )
```

```python
import functools

import jax
import jax.numpy as jnp
from jax import lax
from jax.experimental import pallas as pl
from jax.experimental.pallas import tpu as pltpu
from jax.sharding import Mesh
from jax.sharding import PartitionSpec as P

NY, NX, NZ = 4, 4, 16
NA = 4
F32, BF16 = jnp.float32, jnp.bfloat16
SENDS = 184
PARTS = 7


def body(
    resid, target, enc, bias, dec, blocks,
    x_out, low_out, bias_out, err_out,
    X, XO, XO_T, XS_T, WE, BI, DW, TG, PP, PR, S0, S1, R0, R1, B0, B1, Q0, Q1,
    S2, S2F, R2, YO, YA, YN, YB, E, EM, GP, GR, loc, ssem, rsem,
):
    y, h = lax.axis_index("y"), lax.axis_index("core")
    x, z = lax.axis_index("x"), lax.axis_index("z")
    other = 1 - h
    r, a = lax.rem(z, 4), lax.div(z, 4)
    half = XO.shape[-1]
    width = bias.shape[-1]

    def at_x(d):
        return {"x": lax.rem(x + d, NX)}

    def at_z(d):
        return {"z": lax.rem(z + d + NZ, NZ)}

    sibling = {"core": other}

    barrier = pltpu.get_barrier_semaphore()
    near = [sibling, at_x(1), at_x(2), at_x(3)]
    near += [at_z(d) for d in (1, -1, 2, -2, 3, -3, 4, -4)]
    for peer in near:
        pl.semaphore_signal(barrier, inc=1, device_id=peer, device_id_type=pl.DeviceIdType.MESH)

    @pl.when(y > 0)
    def _():
        pl.semaphore_signal(barrier, inc=1, device_id={"y": y - 1}, device_id_type=pl.DeviceIdType.MESH)

    @pl.when(y < NY - 1)
    def _():
        pl.semaphore_signal(barrier, inc=1, device_id={"y": y + 1}, device_id_type=pl.DeviceIdType.MESH)

    mine = resid.at[y, :, pl.ds(pl.multiple_of(h * half, 128), half)]
    keep = pltpu.make_async_copy(mine, X.at[r, x, a], loc.at[0])
    keep.start()
    enc_own = pltpu.make_async_copy(
        enc.at[0, pl.ds(pl.multiple_of(h * half, 128), half), :],
        WE.at[:, pl.ds(pl.multiple_of(h * width, 128), width)], loc.at[1])
    enc_own.start()
    bias_own = pltpu.make_async_copy(bias, BI.at[h], loc.at[2])
    bias_own.start()
    tgt = pltpu.make_async_copy(
        target.at[pl.ds(y, 2), :, pl.ds(pl.multiple_of(h * half, 128), half)], TG, loc.at[3])
    tgt.start()
    dec_in = pltpu.make_async_copy(dec.at[0], DW, loc.at[4])
    dec_in.start()

    extra = jnp.where(jnp.logical_and(y > 0, y < NY - 1), 2, 1)
    pl.semaphore_wait(barrier, len(near) + extra)

    count = [0]
    started = []

    def made(src, dst, peer):
        k = count[0]
        count[0] += 1
        return pltpu.make_async_remote_copy(
            src_ref=src, dst_ref=dst, send_sem=ssem.at[k], recv_sem=rsem.at[k],
            device_id=peer, device_id_type=pl.DeviceIdType.MESH)

    def send(src, dst, peer):
        copy = made(src, dst, peer)
        copy.start()
        started.append(copy)
        return copy

    def slot(d):
        zz = lax.rem(z + d + NZ, NZ)
        return lax.rem(zz, 4), lax.div(zz, 4)

    def gathered(buf, src):
        own = buf.at[r, x, a]
        out = {d: send(src, own, at_z(d)) for d in (4, -4, 3, -3, 2, -2, 1, -1)}
        across = [send(src, own, at_x(d)) for d in (2, 1, 3)]

        def passed(d):
            rr, aa = slot(-d)
            got = buf.at[rr, x, aa]
            return got, [send(got, got, at_x(dx)) for dx in (2, 1, 3)]

        for d in (1, -1, 2, -2, 3, -3):
            out[d].wait_recv()
            across += passed(d)[1]
        far = {}
        for d, steps in ((4, (4, 3, 2, 1)), (-4, (-3, -2, -1))):
            out[d].wait_recv()
            rr, aa = slot(-d)
            got = buf.at[rr, x, aa]
            for k in steps:
                far[k + d] = send(got, got, at_z(k))
        for d in (4, -4):
            across += passed(d)[1]
        for d in (5, -5, 6, -6, 7, -7, 8):
            far[d].wait_recv()
            across += passed(d)[1]
        return across

    enc_far = send(
        enc.at[0, pl.ds(pl.multiple_of(other * half, 128), half), :],
        WE.at[:, pl.ds(pl.multiple_of(h * width, 128), width)], sibling)
    bias_far = send(bias, BI.at[h], sibling)
    across = gathered(X, mine)

    row = blocks[y]
    column = x * NZ + z
    hits = [
        jnp.max((row == g * NX * NZ + column).astype(F32), axis=1, keepdims=True)
        for g in range(2)
    ]
    lanes = lax.broadcasted_iota(jnp.int32, (1, 2 * width), 1)
    gates = jnp.where(lanes < width, hits[0], hits[1])
    gate_own = jnp.where(h == 0, hits[0], hits[1])

    bias_far.wait_recv()
    bias_own.wait()
    enc_far.wait_recv()
    enc_own.wait()
    keep.wait()
    for copy in across:
        copy.wait_recv()
    for rr in range(4):
        XO[pl.ds(rr * 32, 32), :] = X[rr].reshape(32, half)
    PP[...] = jnp.dot(XO[...], WE[...], preferred_element_type=F32)
    part = send(PP, PR, sibling)
    part.wait_recv()
    biases = jnp.concatenate([BI[0], BI[1]], axis=1)
    acts = ((PP[...] + PR[...] + biases) * gates).astype(BF16)

    dec_in.wait()
    step = 256
    n2 = half // 2
    lo, hi = pl.ds(0, n2), pl.ds(n2, n2)
    r1, r3, r2 = lax.rem(r + 1, 4), lax.rem(r + 3, 4), lax.rem(r + 2, 4)
    classes = ((2, r2), (1, r1), (3, r3), (0, r))
    in1, in0 = {}, {}
    for t, S in ((1, S1), (0, S0)):
        for n in range(0, half, step):
            w = DW[t, :, :, n:n + step].reshape(2 * width, step)
            p = jnp.dot(acts, w, preferred_element_type=F32)
            S[:, :, :, n:n + step] = p.reshape(4, NX, 8, step).astype(BF16)
        if t == 1:
            for d in (2, 1, 3, 0):
                xx = lax.rem(x + d, NX)
                in1[d] = [
                    send(S1.at[r2, xx, :, lo], R1.at[2, xx, :, lo], at_z(2)),
                    send(S1.at[r2, xx, :, hi], R1.at[2, xx, :, hi], at_z(-2)),
                    send(S1.at[r1, xx], R1.at[0, xx], at_z(1)),
                    send(S1.at[r3, xx], R1.at[1, xx], at_z(-1)),
                ]
        else:
            for d, rr in classes:
                in0[d] = [
                    send(S0.at[rr, lax.rem(x + dx, NX)], R0.at[i, rr], at_x(dx))
                    for i, dx in enumerate((2, 1, 3))
                ]
    for n in range(0, half, step):
        XO_T[n:n + step, :] = XO[:, n:n + step].T
    rows_far = send(XO_T, XS_T, sibling)

    def summed1(xx):
        return (S1[r, xx].astype(F32) + R1[0, xx].astype(F32)) + (
            R1[1, xx].astype(F32) + R1[2, xx].astype(F32))

    def summed0(rr):
        return (S0[rr, x].astype(F32) + R0[0, rr].astype(F32)) + (
            R0[1, rr].astype(F32) + R0[2, rr].astype(F32))

    def landed(copies):
        for copy in copies:
            copy.wait_recv()

    after = []
    for i, (d, rr) in enumerate(classes[:3]):
        landed(in1[d])
        B1[i] = summed1(lax.rem(x + d, NX)).astype(BF16)
        after.append(send(B1.at[i], Q1.at[i], at_x(d)))
        landed(in0[d])
        B0[i] = summed0(rr).astype(BF16)
        if d == 2:
            after.append(send(B0.at[i, :, lo], Q0.at[i, :, lo], at_z(2)))
            after.append(send(B0.at[i, :, hi], Q0.at[i, :, hi], at_z(-2)))
        else:
            after.append(send(B0.at[i], Q0.at[i], at_z(1 if d == 1 else -1)))
    landed(in1[0])
    own1 = summed1(x)
    landed(in0[0])
    own0 = summed0(r)
    landed(after)
    for t, own, Q in ((0, own0, Q0), (1, own1, Q1)):
        total = (own + Q[0].astype(F32)) + (Q[1].astype(F32) + Q[2].astype(F32))
        for aa in range(NA):
            two = total[2 * aa:2 * aa + 2, :]
            S2F[aa, t] = two
            S2[aa, t] = two.astype(BF16)
    last = [
        send(S2.at[lax.rem(a + d, NA)], R2.at[i], at_z(4 * d if d < 3 else -4))
        for i, d in enumerate((2, 1, 3))
    ]
    for copy in last:
        copy.wait_recv()
    sums = S2F[a] + R2[0].astype(F32) + R2[1].astype(F32) + R2[2].astype(F32)
    YO[...] = sums[0]
    YA[...] = sums[1]

    up_y = made(YA, YB, {"y": lax.rem(y + 1, NY)})
    down_y = made(YO, YN, {"y": lax.rem(y + NY - 1, NY)})

    @pl.when(y < NY - 1)
    def _():
        up_y.start()

    @pl.when(y > 0)
    def _():
        down_y.start()
        up_y.wait_recv()

    @pl.when(y == 0)
    def _():
        YB[...] = jnp.zeros_like(YB)

    @pl.when(y < NY - 1)
    def _():
        down_y.wait_recv()

    @pl.when(y == NY - 1)
    def _():
        YN[...] = jnp.zeros_like(YN)

    tgt.wait()
    err_own = (sums[0] + YB[...] - TG[0].astype(F32)).astype(BF16)
    err_next = (YN[...] + sums[1] - TG[1].astype(F32)).astype(BF16)
    err_out[0] = err_own
    E[r, x, a, 0] = err_own
    E[r, x, a, 1] = err_next

    rows_far.wait_recv()
    out_a = pltpu.make_async_copy(XO_T, x_out.at[h], loc.at[5])
    out_b = pltpu.make_async_copy(XS_T, x_out.at[other], loc.at[6])
    out_a.start()
    out_b.start()

    for copy in gathered(E, E.at[r, x, a]):
        copy.wait_recv()
    grad = None
    for t in range(2):
        for rr in range(4):
            EM[pl.ds(rr * 32, 32), :] = E[rr, :, :, t].reshape(32, half)
        term = lax.dot_general(
            EM[...], DW[t].reshape(2 * width, half), (((1,), (1,)), ((), ())),
            preferred_element_type=F32)
        grad = term if grad is None else grad + term
    GP[0] = grad[:, :width]
    GP[1] = grad[:, width:]
    back = send(GP.at[other], GR, sibling)

    back.wait_recv()
    grad_pre = (GP[h] + GR[...]) * gate_own
    bias_out[...] = jnp.sum(grad_pre, axis=0, keepdims=True)
    low_out[...] = grad_pre.astype(BF16)
    for copy in started:
        copy.wait_send()

    @pl.when(y < NY - 1)
    def _():
        up_y.wait_send()

    @pl.when(y > 0)
    def _():
        down_y.wait_send()

    out_a.wait()
    out_b.wait()


def on_device(resid, target, enc, bias, dec, blocks):
    half = dec.shape[-1]
    width = enc.shape[-1]
    rows = 128
    hbm = pl.BlockSpec(memory_space=pltpu.HBM)
    vmem = pl.BlockSpec(memory_space=pltpu.VMEM)
    V = pltpu.VMEM
    x_all, low, bias_grad, errors = pl.pallas_call(
        body,
        out_shape=(
            jax.ShapeDtypeStruct((2, half, rows), BF16),
            jax.ShapeDtypeStruct((rows, width), BF16),
            jax.ShapeDtypeStruct((1, width), F32),
            jax.ShapeDtypeStruct((1, 2, half), BF16),
        ),
        in_specs=[hbm] * 5 + [vmem],
        out_specs=(vmem,) * 4,
        scratch_shapes=[
            V((4, NX, NA, 2, half), BF16),
            V((rows, half), BF16),
            V((half, rows), BF16),
            V((half, rows), BF16),
            V((half, 2 * width), BF16),
            V((2, 1, width), F32),
            V((2, 2, width, half), BF16),
            V((2, 2, half), BF16),
            V((rows, 2 * width), F32),
            V((rows, 2 * width), F32),
            V((4, NX, 8, half), BF16),
            V((4, NX, 8, half), BF16),
            V((3, 4, 8, half), BF16),
            V((3, NX, 8, half), BF16),
            V((3, 8, half), BF16),
            V((3, 8, half), BF16),
            V((3, 8, half), BF16),
            V((3, 8, half), BF16),
            V((NA, 2, 2, half), BF16),
            V((NA, 2, 2, half), F32),
            V((3, 2, 2, half), BF16),
            V((2, half), F32),
            V((2, half), F32),
            V((2, half), F32),
            V((2, half), F32),
            V((4, NX, NA, 2, 2, half), BF16),
            V((rows, half), BF16),
            V((2, rows, width), F32),
            V((rows, width), F32),
            pltpu.SemaphoreType.DMA((8,)),
            pltpu.SemaphoreType.DMA((SENDS,)),
            pltpu.SemaphoreType.DMA((SENDS,)),
        ],
        compiler_params=pltpu.CompilerParams(
            collective_id=0, has_side_effects=True, vmem_limit_bytes=53700 << 10),
        name="step",
    )(resid, target, enc, bias, dec, blocks)
    tall = 2 * half // PARTS
    grad, bias_grad, errors = pl.pallas_call(
        weight_gradient,
        out_shape=(
            jax.ShapeDtypeStruct((1, 2 * half, width), BF16),
            jax.ShapeDtypeStruct((1, width), F32),
            jax.ShapeDtypeStruct((1, 2, half), BF16),
        ),
        in_specs=[vmem] * 4,
        out_specs=(hbm, vmem, vmem),
        scratch_shapes=[V((PARTS, tall, width), BF16), pltpu.SemaphoreType.DMA((PARTS,))],
        compiler_params=pltpu.CompilerParams(vmem_limit_bytes=8 << 20),
        name="weights",
    )(x_all.reshape(2 * half, rows), low, bias_grad, errors)
    return errors, grad, bias_grad


def weight_gradient(xt, low, bias_in, err_in, grad, bias_out, err_out, held, sems):
    tall = held.shape[1]
    copies = []
    for i in range(PARTS):
        part = jnp.dot(xt[i * tall:(i + 1) * tall, :], low[...], preferred_element_type=F32)
        held[i] = part.astype(BF16)
        copies.append(pltpu.make_async_copy(
            held.at[i], grad.at[0, pl.ds(i * tall, tall), :], sems.at[i]))
        copies[-1].start()
    bias_out[...] = bias_in[...]
    err_out[...] = err_in[...]
    for copy in copies:
        copy.wait()


def solution(mesh):
    fine = Mesh(mesh.devices.reshape(NY, 2, NX, NZ), ("y", "core", "x", "z"))
    layer, latent = ("y", "core"), ("x", "z")
    return jax.shard_map(
        on_device,
        mesh=fine,
        in_specs=(
            P(None, latent, None), P(None, latent, None), P(layer, None, latent),
            P(layer, latent), P(layer, None, None, latent, None), P(),
        ),
        out_specs=(P(layer, latent, None), P(layer, None, latent), P(layer, latent)),
        check_vma=False,
    )
```

```python
import functools

import jax
import jax.numpy as jnp
from jax import lax
from jax.experimental import pallas as pl
from jax.experimental.pallas import tpu as pltpu
from jax.sharding import Mesh
from jax.sharding import PartitionSpec as P

NY, NX, NZ = 4, 4, 16
NA = 4
F32, BF16 = jnp.float32, jnp.bfloat16
SENDS = 200
PARTS = 7


def body(
    resid, target, enc, bias, dec, blocks,
    x_out, low_out, bias_out, err_out,
    X, XO, XO_T, XS_T, WE, BI, DW, TG, PP, PR, S0, S1, R0, R1, B0, B1, Q0, Q1,
    S2, S2F, R2, YO, YA, YN, YB, E, EM, GP, GR, BK, loc, ssem, rsem,
):
    y, h = lax.axis_index("y"), lax.axis_index("core")
    x, z = lax.axis_index("x"), lax.axis_index("z")
    other = 1 - h
    r, a = lax.rem(z, 4), lax.div(z, 4)
    half = XO.shape[-1]
    width = bias.shape[-1]

    def at_x(d):
        return {"x": lax.rem(x + d, NX)}

    def at_z(d):
        return {"z": lax.rem(z + d + NZ, NZ)}

    sibling = {"core": other}

    barrier = pltpu.get_barrier_semaphore()
    near = [sibling, at_x(1), at_x(2), at_x(3)]
    near += [at_z(d) for d in (1, -1, 2, -2, 3, -3, 4, -4)]
    for peer in near:
        pl.semaphore_signal(barrier, inc=1, device_id=peer, device_id_type=pl.DeviceIdType.MESH)

    @pl.when(y > 0)
    def _():
        pl.semaphore_signal(barrier, inc=1, device_id={"y": y - 1}, device_id_type=pl.DeviceIdType.MESH)

    @pl.when(y < NY - 1)
    def _():
        pl.semaphore_signal(barrier, inc=1, device_id={"y": y + 1}, device_id_type=pl.DeviceIdType.MESH)

    mine = resid.at[y, :, pl.ds(pl.multiple_of(h * half, 128), half)]
    keep = pltpu.make_async_copy(mine, X.at[r, x, a], loc.at[0])
    keep.start()
    enc_own = pltpu.make_async_copy(
        enc.at[0, pl.ds(pl.multiple_of(h * half, 128), half), :],
        WE.at[:, pl.ds(pl.multiple_of(h * width, 128), width)], loc.at[1])
    enc_own.start()
    bias_own = pltpu.make_async_copy(bias, BI.at[h], loc.at[2])
    bias_own.start()
    tgt = pltpu.make_async_copy(
        target.at[pl.ds(y, 2), :, pl.ds(pl.multiple_of(h * half, 128), half)], TG, loc.at[3])
    tgt.start()
    dec_in = pltpu.make_async_copy(dec.at[0], DW, loc.at[4])
    dec_in.start()

    fire = pltpu.make_async_copy(blocks, BK, loc.at[7])
    fire.start()
    extra = jnp.where(jnp.logical_and(y > 0, y < NY - 1), 2, 1)
    pl.semaphore_wait(barrier, len(near) + extra)

    count = [0]
    started = []

    def made(src, dst, peer):
        k = count[0]
        count[0] += 1
        return pltpu.make_async_remote_copy(
            src_ref=src, dst_ref=dst, send_sem=ssem.at[k], recv_sem=rsem.at[k],
            device_id=peer, device_id_type=pl.DeviceIdType.MESH)

    def send(src, dst, peer):
        copy = made(src, dst, peer)
        copy.start()
        started.append(copy)
        return copy

    def slot(d):
        zz = lax.rem(z + d + NZ, NZ)
        return lax.rem(zz, 4), lax.div(zz, 4)

    def gathered(buf, src):
        own = buf.at[r, x, a]
        out = {d: send(src, own, at_z(d)) for d in (4, -4, 3, -3, 2, -2, 1, -1)}
        across = [send(src, own, at_x(d)) for d in (2, 1, 3)]

        def passed(d):
            rr, aa = slot(-d)
            got = buf.at[rr, x, aa]
            return got, [send(got, got, at_x(dx)) for dx in (2, 1, 3)]

        for d in (1, -1, 2, -2, 3, -3):
            out[d].wait_recv()
            across += passed(d)[1]
        far = {}
        for d, steps in ((4, (4, 3, 2, 1)), (-4, (-3, -2, -1))):
            out[d].wait_recv()
            rr, aa = slot(-d)
            got = buf.at[rr, x, aa]
            for k in steps:
                far[k + d] = send(got, got, at_z(k))
        for d in (4, -4):
            across += passed(d)[1]
        for d in (5, -5, 6, -6, 7, -7, 8):
            far[d].wait_recv()
            across += passed(d)[1]
        return across

    def gathered_pairs(buf):
        own = buf.at[r, x, a]
        out = {d: send(own, own, at_z(d)) for d in (4, -4, 3, -3, 2, -2, 1, -1)}
        left, right = lax.rem(x + 3, NX), lax.rem(x + 1, NX)
        beside = {}
        rest = []

        def to_sides(d):
            rr, aa = slot(-d)
            got = buf.at[rr, x, aa]
            beside[d] = (send(got, got, at_x(1)), send(got, got, at_x(3)))

        def relayed(d):
            rr, aa = slot(-d)
            beside[d][0].wait_recv()
            first = buf.at[rr, left, aa, 0]
            beside[d][1].wait_recv()
            second = buf.at[rr, right, aa, 1]
            return [send(first, first, at_x(1)), send(second, second, at_x(3))]

        def to_next(xx):
            got = buf.at[r, xx, a]
            return [send(got, got, at_z(d)) for d in (1, -1)]

        def to_all(d):
            far[d].wait_recv()
            rr, aa = slot(-d)
            got = buf.at[rr, x, aa]
            return [send(got, got, at_x(dx)) for dx in (2, 1, 3)]

        to_sides(0)
        for d in (2, -2):
            out[d].wait_recv()
            to_sides(d)
        opposite = relayed(0)
        rest += to_next(left) + to_next(right)
        far = {}
        for d, steps in ((4, (4, 3, 2, 1)), (-4, (-3, -2, -1))):
            out[d].wait_recv()
            rr, aa = slot(-d)
            got = buf.at[rr, x, aa]
            for k in steps:
                far[k + d] = send(got, got, at_z(k))
        for d in (3, -3):
            out[d].wait_recv()
            to_sides(d)
        for d in (4, -4):
            to_sides(d)
        for d in (2, -2):
            rest += relayed(d)
        for copy in opposite:
            copy.wait_recv()
        rest += to_next(lax.rem(x + 2, NX))
        for d in (5, -5):
            rest += to_all(d)
        for d in (3, -3):
            rest += relayed(d)
        for d in (6, -6):
            rest += to_all(d)
        for d in (4, -4):
            rest += relayed(d)
        for d in (7, -7, 8):
            rest += to_all(d)
        return rest + [out[1], out[-1]]

    enc_far = send(
        enc.at[0, pl.ds(pl.multiple_of(other * half, 128), half), :],
        WE.at[:, pl.ds(pl.multiple_of(h * width, 128), width)], sibling)
    bias_far = send(bias, BI.at[h], sibling)
    across = gathered(X, mine)

    fire.wait()
    row = BK[y]
    column = x * NZ + z
    hits = [
        jnp.max((row == g * NX * NZ + column).astype(F32), axis=1, keepdims=True)
        for g in range(2)
    ]
    lanes = lax.broadcasted_iota(jnp.int32, (1, 2 * width), 1)
    gates = jnp.where(lanes < width, hits[0], hits[1])
    gate_own = jnp.where(h == 0, hits[0], hits[1])

    bias_far.wait_recv()
    bias_own.wait()
    enc_far.wait_recv()
    enc_own.wait()
    keep.wait()
    for copy in across:
        copy.wait_recv()
    for rr in range(4):
        XO[pl.ds(rr * 32, 32), :] = X[rr].reshape(32, half)
    PP[...] = jnp.dot(XO[...], WE[...], preferred_element_type=F32)
    part = send(PP, PR, sibling)
    part.wait_recv()
    biases = jnp.concatenate([BI[0], BI[1]], axis=1)
    acts = ((PP[...] + PR[...] + biases) * gates).astype(BF16)

    dec_in.wait()
    step = 256
    n2 = half // 2
    lo, hi = pl.ds(0, n2), pl.ds(n2, n2)
    r1, r3, r2 = lax.rem(r + 1, 4), lax.rem(r + 3, 4), lax.rem(r + 2, 4)
    classes = ((2, r2), (1, r1), (3, r3), (0, r))
    in1, in0 = {}, {}
    for t, S in ((1, S1), (0, S0)):
        for n in range(0, half, step):
            w = DW[t, :, :, n:n + step].reshape(2 * width, step)
            p = jnp.dot(acts, w, preferred_element_type=F32)
            S[:, :, :, n:n + step] = p.reshape(4, NX, 8, step).astype(BF16)
        if t == 1:
            for d in (2, 1, 3, 0):
                xx = lax.rem(x + d, NX)
                in1[d] = [
                    send(S1.at[r2, xx, :, lo], R1.at[2, xx, :, lo], at_z(2)),
                    send(S1.at[r2, xx, :, hi], R1.at[2, xx, :, hi], at_z(-2)),
                    send(S1.at[r1, xx], R1.at[0, xx], at_z(1)),
                    send(S1.at[r3, xx], R1.at[1, xx], at_z(-1)),
                ]
        else:
            for d, rr in classes:
                in0[d] = [
                    send(S0.at[rr, lax.rem(x + dx, NX)], R0.at[i, rr], at_x(dx))
                    for i, dx in enumerate((2, 1, 3))
                ]
    for n in range(0, half, step):
        XO_T[n:n + step, :] = XO[:, n:n + step].T
    rows_far = send(XO_T, XS_T, sibling)

    def summed1(xx):
        return (S1[r, xx].astype(F32) + R1[0, xx].astype(F32)) + (
            R1[1, xx].astype(F32) + R1[2, xx].astype(F32))

    def summed0(rr):
        return (S0[rr, x].astype(F32) + R0[0, rr].astype(F32)) + (
            R0[1, rr].astype(F32) + R0[2, rr].astype(F32))

    def landed(copies):
        for copy in copies:
            copy.wait_recv()

    after = []
    for i, (d, rr) in enumerate(classes[:3]):
        landed(in1[d])
        B1[i] = summed1(lax.rem(x + d, NX)).astype(BF16)
        after.append(send(B1.at[i], Q1.at[i], at_x(d)))
        landed(in0[d])
        B0[i] = summed0(rr).astype(BF16)
        if d == 2:
            after.append(send(B0.at[i, :, lo], Q0.at[i, :, lo], at_z(2)))
            after.append(send(B0.at[i, :, hi], Q0.at[i, :, hi], at_z(-2)))
        else:
            after.append(send(B0.at[i], Q0.at[i], at_z(1 if d == 1 else -1)))
    landed(in1[0])
    own1 = summed1(x)
    landed(in0[0])
    own0 = summed0(r)
    landed(after)
    for t, own, Q in ((0, own0, Q0), (1, own1, Q1)):
        total = (own + Q[0].astype(F32)) + (Q[1].astype(F32) + Q[2].astype(F32))
        for aa in range(NA):
            two = total[2 * aa:2 * aa + 2, :]
            S2F[aa, t] = two
            S2[aa, t] = two.astype(BF16)
    last = [
        send(S2.at[lax.rem(a + d, NA)], R2.at[i], at_z(4 * d if d < 3 else -4))
        for i, d in enumerate((2, 1, 3))
    ]
    for copy in last:
        copy.wait_recv()
    sums = S2F[a] + R2[0].astype(F32) + R2[1].astype(F32) + R2[2].astype(F32)
    YO[...] = sums[0]
    YA[...] = sums[1]

    up_y = made(YA, YB, {"y": lax.rem(y + 1, NY)})
    down_y = made(YO, YN, {"y": lax.rem(y + NY - 1, NY)})

    @pl.when(y < NY - 1)
    def _():
        up_y.start()

    @pl.when(y > 0)
    def _():
        down_y.start()
        up_y.wait_recv()

    @pl.when(y == 0)
    def _():
        YB[...] = jnp.zeros_like(YB)

    @pl.when(y < NY - 1)
    def _():
        down_y.wait_recv()

    @pl.when(y == NY - 1)
    def _():
        YN[...] = jnp.zeros_like(YN)

    tgt.wait()
    err_own = (sums[0] + YB[...] - TG[0].astype(F32)).astype(BF16)
    err_next = (YN[...] + sums[1] - TG[1].astype(F32)).astype(BF16)
    err_out[0] = err_own
    E[r, x, a, 0] = err_own
    E[r, x, a, 1] = err_next

    rows_far.wait_recv()
    out_a = pltpu.make_async_copy(XO_T, x_out.at[h], loc.at[5])
    out_b = pltpu.make_async_copy(XS_T, x_out.at[other], loc.at[6])
    out_a.start()
    out_b.start()

    for copy in gathered_pairs(E):
        copy.wait_recv()
    for t in range(2):
        for rr in range(4):
            EM[t, pl.ds(rr * 32, 32), :] = E[rr, :, :, t].reshape(32, half)

    def latent_grad(g):
        terms = [
            lax.dot_general(
                EM[t], DW[t, g], (((1,), (1,)), ((), ())), preferred_element_type=F32)
            for t in range(2)
        ]
        return terms[0] + terms[1]

    GP[...] = latent_grad(other)
    back = send(GP, GR, sibling)
    grad_own = latent_grad(h)
    back.wait_recv()
    grad_pre = (grad_own + GR[...]) * gate_own
    bias_out[...] = jnp.sum(grad_pre, axis=0, keepdims=True)
    low_out[...] = grad_pre.astype(BF16)
    for copy in started:
        copy.wait_send()

    @pl.when(y < NY - 1)
    def _():
        up_y.wait_send()

    @pl.when(y > 0)
    def _():
        down_y.wait_send()

    out_a.wait()
    out_b.wait()


def on_device(resid, target, enc, bias, dec, blocks):
    half = dec.shape[-1]
    width = enc.shape[-1]
    rows = 128
    hbm = pl.BlockSpec(memory_space=pltpu.HBM)
    vmem = pl.BlockSpec(memory_space=pltpu.VMEM)
    V = pltpu.VMEM
    resid, target, enc, bias, dec, blocks = (
        pltpu.with_memory_space_constraint(v, pltpu.HBM)
        for v in (resid, target, enc, bias, dec, blocks))
    x_all, low, bias_grad, errors = pl.pallas_call(
        body,
        out_shape=(
            jax.ShapeDtypeStruct((2, half, rows), BF16),
            jax.ShapeDtypeStruct((rows, width), BF16),
            jax.ShapeDtypeStruct((1, width), F32),
            jax.ShapeDtypeStruct((1, 2, half), BF16),
        ),
        in_specs=[hbm] * 6,
        out_specs=(vmem,) * 4,
        scratch_shapes=[
            V((4, NX, NA, 2, half), BF16),
            V((rows, half), BF16),
            V((half, rows), BF16),
            V((half, rows), BF16),
            V((half, 2 * width), BF16),
            V((2, 1, width), F32),
            V((2, 2, width, half), BF16),
            V((2, 2, half), BF16),
            V((rows, 2 * width), F32),
            V((rows, 2 * width), F32),
            V((4, NX, 8, half), BF16),
            V((4, NX, 8, half), BF16),
            V((3, 4, 8, half), BF16),
            V((3, NX, 8, half), BF16),
            V((3, 8, half), BF16),
            V((3, 8, half), BF16),
            V((3, 8, half), BF16),
            V((3, 8, half), BF16),
            V((NA, 2, 2, half), BF16),
            V((NA, 2, 2, half), F32),
            V((3, 2, 2, half), BF16),
            V((2, half), F32),
            V((2, half), F32),
            V((2, half), F32),
            V((2, half), F32),
            V((4, NX, NA, 2, 2, half), BF16),
            V((2, rows, half), BF16),
            V((rows, width), F32),
            V((rows, width), F32),
            V(blocks.shape, jnp.int32),
            pltpu.SemaphoreType.DMA((8,)),
            pltpu.SemaphoreType.DMA((SENDS,)),
            pltpu.SemaphoreType.DMA((SENDS,)),
        ],
        compiler_params=pltpu.CompilerParams(
            collective_id=0, has_side_effects=True, vmem_limit_bytes=53700 << 10),
        name="step",
    )(resid, target, enc, bias, dec, blocks)
    tall = 2 * half // PARTS
    grad, bias_grad, errors = pl.pallas_call(
        weight_gradient,
        out_shape=(
            jax.ShapeDtypeStruct((1, 2 * half, width), BF16),
            jax.ShapeDtypeStruct((1, width), F32),
            jax.ShapeDtypeStruct((1, 2, half), BF16),
        ),
        in_specs=[vmem] * 4,
        out_specs=(hbm, vmem, vmem),
        scratch_shapes=[V((PARTS, tall, width), BF16), pltpu.SemaphoreType.DMA((PARTS,))],
        compiler_params=pltpu.CompilerParams(vmem_limit_bytes=8 << 20),
        name="weights",
    )(x_all.reshape(2 * half, rows), low, bias_grad, errors)
    return errors, grad, bias_grad


def weight_gradient(xt, low, bias_in, err_in, grad, bias_out, err_out, held, sems):
    tall = held.shape[1]
    copies = []
    for i in range(PARTS):
        part = jnp.dot(xt[i * tall:(i + 1) * tall, :], low[...], preferred_element_type=F32)
        held[i] = part.astype(BF16)
        copies.append(pltpu.make_async_copy(
            held.at[i], grad.at[0, pl.ds(i * tall, tall), :], sems.at[i]))
        copies[-1].start()
    bias_out[...] = bias_in[...]
    err_out[...] = err_in[...]
    for copy in copies:
        copy.wait()


def solution(mesh):
    fine = Mesh(mesh.devices.reshape(NY, 2, NX, NZ), ("y", "core", "x", "z"))
    layer, latent = ("y", "core"), ("x", "z")
    return jax.shard_map(
        on_device,
        mesh=fine,
        in_specs=(
            P(None, latent, None), P(None, latent, None), P(layer, None, latent),
            P(layer, latent), P(layer, None, None, latent, None), P(),
        ),
        out_specs=(P(layer, latent, None), P(layer, None, latent), P(layer, latent)),
        check_vma=False,
    )
```

```python
import functools

import jax
import jax.numpy as jnp
from jax import lax
from jax.experimental import pallas as pl
from jax.experimental.pallas import tpu as pltpu
from jax.sharding import Mesh
from jax.sharding import PartitionSpec as P

NY, NX, NZ = 4, 4, 16
NA = 4
F32, BF16 = jnp.float32, jnp.bfloat16
SENDS = 216
PARTS = 7


def body(
    resid, target, enc, bias, dec, blocks,
    x_out, low_out, bias_out, err_out,
    X, XO, XO_T, XS_T, WE, BI, DW, TG, PP, PR, S0, S1, R0, R1, B0, B1, Q0, Q1,
    S2, S2F, R2, QN, QB, E, EM, GP, GR, BK, loc, ssem, rsem,
):
    y, h = lax.axis_index("y"), lax.axis_index("core")
    x, z = lax.axis_index("x"), lax.axis_index("z")
    other = 1 - h
    r, a = lax.rem(z, 4), lax.div(z, 4)
    half = XO.shape[-1]
    width = bias.shape[-1]

    def at_x(d):
        return {"x": lax.rem(x + d, NX)}

    def at_z(d):
        return {"z": lax.rem(z + d + NZ, NZ)}

    sibling = {"core": other}

    barrier = pltpu.get_barrier_semaphore()
    near = [sibling, at_x(1), at_x(2), at_x(3)]
    near += [at_z(d) for d in (1, -1, 2, -2, 3, -3, 4, -4)]
    for peer in near:
        pl.semaphore_signal(barrier, inc=1, device_id=peer, device_id_type=pl.DeviceIdType.MESH)

    def greet(peers):
        for peer in peers:
            pl.semaphore_signal(
                barrier, inc=1, device_id=peer, device_id_type=pl.DeviceIdType.MESH)

    @pl.when(y > 0)
    def _():
        greet([{"y": y - 1}] + [{"y": y - 1, **at_x(d)} for d in (1, 2, 3)])

    @pl.when(y < NY - 1)
    def _():
        greet([{"y": y + 1}] + [{"y": y + 1, **at_z(d)} for d in (1, -1, 2, -2)])

    @pl.when(y == 0)
    def _():
        QB[...] = jnp.zeros_like(QB)

    @pl.when(y == NY - 1)
    def _():
        QN[...] = jnp.zeros_like(QN)

    mine = resid.at[y, :, pl.ds(pl.multiple_of(h * half, 128), half)]
    keep = pltpu.make_async_copy(mine, X.at[r, x, a], loc.at[0])
    keep.start()
    enc_own = pltpu.make_async_copy(
        enc.at[0, pl.ds(pl.multiple_of(h * half, 128), half), :],
        WE.at[:, pl.ds(pl.multiple_of(h * width, 128), width)], loc.at[1])
    enc_own.start()
    bias_own = pltpu.make_async_copy(bias, BI.at[h], loc.at[2])
    bias_own.start()
    tgt = pltpu.make_async_copy(
        target.at[pl.ds(y, 2), :, pl.ds(pl.multiple_of(h * half, 128), half)], TG, loc.at[3])
    tgt.start()
    dec_in = pltpu.make_async_copy(dec.at[0], DW, loc.at[4])
    dec_in.start()

    fire = pltpu.make_async_copy(blocks, BK, loc.at[7])
    fire.start()
    extra = jnp.where(y < NY - 1, 4, 0) + jnp.where(y > 0, 5, 0)
    pl.semaphore_wait(barrier, len(near) + extra)

    count = [0]
    started = []

    def made(src, dst, peer):
        k = count[0]
        count[0] += 1
        return pltpu.make_async_remote_copy(
            src_ref=src, dst_ref=dst, send_sem=ssem.at[k], recv_sem=rsem.at[k],
            device_id=peer, device_id_type=pl.DeviceIdType.MESH)

    def send(src, dst, peer):
        copy = made(src, dst, peer)
        copy.start()
        started.append(copy)
        return copy

    def slot(d):
        zz = lax.rem(z + d + NZ, NZ)
        return lax.rem(zz, 4), lax.div(zz, 4)

    def gathered(buf, src):
        own = buf.at[r, x, a]
        out = {d: send(src, own, at_z(d)) for d in (4, -4, 3, -3, 2, -2, 1, -1)}
        across = [send(src, own, at_x(d)) for d in (2, 1, 3)]

        def passed(d):
            rr, aa = slot(-d)
            got = buf.at[rr, x, aa]
            return got, [send(got, got, at_x(dx)) for dx in (2, 1, 3)]

        for d in (1, -1, 2, -2, 3, -3):
            out[d].wait_recv()
            across += passed(d)[1]
        far = {}
        for d, steps in ((4, (4, 3, 2, 1)), (-4, (-3, -2, -1))):
            out[d].wait_recv()
            rr, aa = slot(-d)
            got = buf.at[rr, x, aa]
            for k in steps:
                far[k + d] = send(got, got, at_z(k))
        for d in (4, -4):
            across += passed(d)[1]
        for d in (5, -5, 6, -6, 7, -7, 8):
            far[d].wait_recv()
            across += passed(d)[1]
        return across

    enc_far = send(
        enc.at[0, pl.ds(pl.multiple_of(other * half, 128), half), :],
        WE.at[:, pl.ds(pl.multiple_of(h * width, 128), width)], sibling)
    bias_far = send(bias, BI.at[h], sibling)
    across = gathered(X, mine)

    fire.wait()
    row = BK[y]
    column = x * NZ + z
    hits = [
        jnp.max((row == g * NX * NZ + column).astype(F32), axis=1, keepdims=True)
        for g in range(2)
    ]
    lanes = lax.broadcasted_iota(jnp.int32, (1, 2 * width), 1)
    gates = jnp.where(lanes < width, hits[0], hits[1])
    gate_own = jnp.where(h == 0, hits[0], hits[1])

    bias_far.wait_recv()
    bias_own.wait()
    enc_far.wait_recv()
    enc_own.wait()
    keep.wait()
    for copy in across:
        copy.wait_recv()
    for rr in range(4):
        XO[pl.ds(rr * 32, 32), :] = X[rr].reshape(32, half)
    PP[...] = jnp.dot(XO[...], WE[...], preferred_element_type=F32)
    part = send(PP, PR, sibling)
    part.wait_recv()
    biases = jnp.concatenate([BI[0], BI[1]], axis=1)
    acts = ((PP[...] + PR[...] + biases) * gates).astype(BF16)

    dec_in.wait()
    step = 256
    n2 = half // 2
    lo, hi = pl.ds(0, n2), pl.ds(n2, n2)
    r1, r3, r2 = lax.rem(r + 1, 4), lax.rem(r + 3, 4), lax.rem(r + 2, 4)
    classes = ((2, r2), (1, r1), (3, r3), (0, r))
    in1, in0 = {}, {}
    for t, S in ((1, S1), (0, S0)):
        for n in range(0, half, step):
            w = DW[t, :, :, n:n + step].reshape(2 * width, step)
            p = jnp.dot(acts, w, preferred_element_type=F32)
            S[:, :, :, n:n + step] = p.reshape(4, NX, 8, step).astype(BF16)
        if t == 1:
            for d in (2, 1, 3, 0):
                xx = lax.rem(x + d, NX)
                in1[d] = [
                    send(S1.at[r2, xx, :, lo], R1.at[2, xx, :, lo], at_z(2)),
                    send(S1.at[r2, xx, :, hi], R1.at[2, xx, :, hi], at_z(-2)),
                    send(S1.at[r1, xx], R1.at[0, xx], at_z(1)),
                    send(S1.at[r3, xx], R1.at[1, xx], at_z(-1)),
                ]
        else:
            for d, rr in classes:
                in0[d] = [
                    send(S0.at[rr, lax.rem(x + dx, NX)], R0.at[i, rr], at_x(dx))
                    for i, dx in enumerate((2, 1, 3))
                ]
    for n in range(0, half, step):
        XO_T[n:n + step, :] = XO[:, n:n + step].T
    rows_far = send(XO_T, XS_T, sibling)

    def summed1(xx):
        return (S1[r, xx].astype(F32) + R1[0, xx].astype(F32)) + (
            R1[1, xx].astype(F32) + R1[2, xx].astype(F32))

    def summed0(rr):
        return (S0[rr, x].astype(F32) + R0[0, rr].astype(F32)) + (
            R0[1, rr].astype(F32) + R0[2, rr].astype(F32))

    def landed(copies):
        for copy in copies:
            copy.wait_recv()

    after, above, below = [], [], []
    up_y = {"y": lax.rem(y + 1, NY)}
    down_y = {"y": lax.rem(y + NY - 1, NY)}

    def start_above(*copies):
        above.extend(copies)

        @pl.when(y < NY - 1)
        def _():
            for copy in copies:
                copy.start()

    def start_below(*copies):
        below.extend(copies)

        @pl.when(y > 0)
        def _():
            for copy in copies:
                copy.start()

    for i, (d, rr) in enumerate(classes[:3]):
        landed(in1[d])
        B1[i] = summed1(lax.rem(x + d, NX)).astype(BF16)
        start_above(made(B1.at[i], QB.at[i], {**up_y, **at_x(d)}))
        after.append(send(B1.at[i], Q1.at[i], at_x(d)))
        landed(in0[d])
        B0[i] = summed0(rr).astype(BF16)
        if d == 2:
            parts = ((lo, at_z(2)), (hi, at_z(-2)))
            start_below(*[
                made(B0.at[i, :, cols], QN.at[i, :, cols], {**down_y, **to})
                for cols, to in parts
            ])
            after += [send(B0.at[i, :, cols], Q0.at[i, :, cols], to) for cols, to in parts]
        else:
            to = at_z(1 if d == 1 else -1)
            start_below(made(B0.at[i], QN.at[i], {**down_y, **to}))
            after.append(send(B0.at[i], Q0.at[i], to))
    landed(in1[0])
    own1 = summed1(x)
    B1[3] = own1.astype(BF16)
    start_above(made(B1.at[3], QB.at[3], up_y))
    landed(in0[0])
    own0 = summed0(r)
    B0[3] = own0.astype(BF16)
    start_below(made(B0.at[3], QN.at[3], down_y))
    landed(after)

    @pl.when(y > 0)
    def _():
        landed(above)

    @pl.when(y < NY - 1)
    def _():
        landed(below)

    for t, own, Q, QY in ((0, own0, Q0, QB), (1, own1, Q1, QN)):
        total = (own + Q[0].astype(F32)) + (Q[1].astype(F32) + Q[2].astype(F32))
        total = total + (
            (QY[0].astype(F32) + QY[1].astype(F32)) + (QY[2].astype(F32) + QY[3].astype(F32)))
        for aa in range(NA):
            two = total[2 * aa:2 * aa + 2, :]
            S2F[aa, t] = two
            S2[aa, t] = two.astype(BF16)
    last = [
        send(S2.at[lax.rem(a + d, NA)], R2.at[i], at_z(4 * d if d < 3 else -4))
        for i, d in enumerate((2, 1, 3))
    ]
    for copy in last:
        copy.wait_recv()
    sums = S2F[a] + R2[0].astype(F32) + R2[1].astype(F32) + R2[2].astype(F32)

    tgt.wait()
    err_own = (sums[0] - TG[0].astype(F32)).astype(BF16)
    err_next = (sums[1] - TG[1].astype(F32)).astype(BF16)
    err_out[0] = err_own
    E[r, x, a, 0] = err_own
    E[r, x, a, 1] = err_next

    rows_far.wait_recv()
    out_a = pltpu.make_async_copy(XO_T, x_out.at[h], loc.at[5])
    out_b = pltpu.make_async_copy(XS_T, x_out.at[other], loc.at[6])
    out_a.start()
    out_b.start()

    for copy in gathered(E, E.at[r, x, a]):
        copy.wait_recv()
    for t in range(2):
        for rr in range(4):
            EM[t, pl.ds(rr * 32, 32), :] = E[rr, :, :, t].reshape(32, half)

    def latent_grad(g):
        terms = [
            lax.dot_general(
                EM[t], DW[t, g], (((1,), (1,)), ((), ())), preferred_element_type=F32)
            for t in range(2)
        ]
        return terms[0] + terms[1]

    GP[...] = latent_grad(other)
    back = send(GP, GR, sibling)
    grad_own = latent_grad(h)
    back.wait_recv()
    grad_pre = (grad_own + GR[...]) * gate_own
    bias_out[...] = jnp.sum(grad_pre, axis=0, keepdims=True)
    low_out[...] = grad_pre.astype(BF16)
    for copy in started:
        copy.wait_send()

    @pl.when(y < NY - 1)
    def _():
        for copy in above:
            copy.wait_send()

    @pl.when(y > 0)
    def _():
        for copy in below:
            copy.wait_send()

    out_a.wait()
    out_b.wait()


def on_device(resid, target, enc, bias, dec, blocks):
    half = dec.shape[-1]
    width = enc.shape[-1]
    rows = 128
    hbm = pl.BlockSpec(memory_space=pltpu.HBM)
    vmem = pl.BlockSpec(memory_space=pltpu.VMEM)
    V = pltpu.VMEM
    resid, target, enc, bias, dec, blocks = (
        pltpu.with_memory_space_constraint(v, pltpu.HBM)
        for v in (resid, target, enc, bias, dec, blocks))
    x_all, low, bias_grad, errors = pl.pallas_call(
        body,
        out_shape=(
            jax.ShapeDtypeStruct((2, half, rows), BF16),
            jax.ShapeDtypeStruct((rows, width), BF16),
            jax.ShapeDtypeStruct((1, width), F32),
            jax.ShapeDtypeStruct((1, 2, half), BF16),
        ),
        in_specs=[hbm] * 6,
        out_specs=(vmem,) * 4,
        scratch_shapes=[
            V((4, NX, NA, 2, half), BF16),
            V((rows, half), BF16),
            V((half, rows), BF16),
            V((half, rows), BF16),
            V((half, 2 * width), BF16),
            V((2, 1, width), F32),
            V((2, 2, width, half), BF16),
            V((2, 2, half), BF16),
            V((rows, 2 * width), F32),
            V((rows, 2 * width), F32),
            V((4, NX, 8, half), BF16),
            V((4, NX, 8, half), BF16),
            V((3, 4, 8, half), BF16),
            V((3, NX, 8, half), BF16),
            V((4, 8, half), BF16),
            V((4, 8, half), BF16),
            V((3, 8, half), BF16),
            V((3, 8, half), BF16),
            V((NA, 2, 2, half), BF16),
            V((NA, 2, 2, half), F32),
            V((3, 2, 2, half), BF16),
            V((4, 8, half), BF16),
            V((4, 8, half), BF16),
            V((4, NX, NA, 2, 2, half), BF16),
            V((2, rows, half), BF16),
            V((rows, width), F32),
            V((rows, width), F32),
            V(blocks.shape, jnp.int32),
            pltpu.SemaphoreType.DMA((8,)),
            pltpu.SemaphoreType.DMA((SENDS,)),
            pltpu.SemaphoreType.DMA((SENDS,)),
        ],
        compiler_params=pltpu.CompilerParams(
            collective_id=0, has_side_effects=True, vmem_limit_bytes=53700 << 10),
        name="step",
    )(resid, target, enc, bias, dec, blocks)
    tall = 2 * half // PARTS
    grad, bias_grad, errors = pl.pallas_call(
        weight_gradient,
        out_shape=(
            jax.ShapeDtypeStruct((1, 2 * half, width), BF16),
            jax.ShapeDtypeStruct((1, width), F32),
            jax.ShapeDtypeStruct((1, 2, half), BF16),
        ),
        in_specs=[vmem] * 4,
        out_specs=(hbm, vmem, vmem),
        scratch_shapes=[V((PARTS, tall, width), BF16), pltpu.SemaphoreType.DMA((PARTS,))],
        compiler_params=pltpu.CompilerParams(vmem_limit_bytes=8 << 20),
        name="weights",
    )(x_all.reshape(2 * half, rows), low, bias_grad, errors)
    return errors, grad, bias_grad


def weight_gradient(xt, low, bias_in, err_in, grad, bias_out, err_out, held, sems):
    tall = held.shape[1]
    copies = []
    for i in range(PARTS):
        part = jnp.dot(xt[i * tall:(i + 1) * tall, :], low[...], preferred_element_type=F32)
        held[i] = part.astype(BF16)
        copies.append(pltpu.make_async_copy(
            held.at[i], grad.at[0, pl.ds(i * tall, tall), :], sems.at[i]))
        copies[-1].start()
    bias_out[...] = bias_in[...]
    err_out[...] = err_in[...]
    for copy in copies:
        copy.wait()


def solution(mesh):
    fine = Mesh(mesh.devices.reshape(NY, 2, NX, NZ), ("y", "core", "x", "z"))
    layer, latent = ("y", "core"), ("x", "z")
    return jax.shard_map(
        on_device,
        mesh=fine,
        in_specs=(
            P(None, latent, None), P(None, latent, None), P(layer, None, latent),
            P(layer, latent), P(layer, None, None, latent, None), P(),
        ),
        out_specs=(P(layer, latent, None), P(layer, None, latent), P(layer, latent)),
        check_vma=False,
    )
```

```python
import functools

import jax
import jax.numpy as jnp
from jax import lax
from jax.experimental import pallas as pl
from jax.experimental.pallas import tpu as pltpu
from jax.sharding import Mesh
from jax.sharding import PartitionSpec as P

NY, NX, NZ = 4, 4, 16
NA = 4
F32, BF16 = jnp.float32, jnp.bfloat16
SENDS = 216
PARTS = 7


def body(
    resid, target, enc, bias, dec, blocks,
    x_out, low_out, bias_out, err_out,
    X, XO, XS_T, WE, BI, DW, TG, PP, PR, S0, S1, R0, R1, B0, B1, Q0, Q1,
    S2, S2F, R2, QN, QB, E, EM, GP, GR, BK, loc, ssem, rsem,
):
    y, h = lax.axis_index("y"), lax.axis_index("core")
    x, z = lax.axis_index("x"), lax.axis_index("z")
    other = 1 - h
    r, a = lax.rem(z, 4), lax.div(z, 4)
    half = XO.shape[-1]
    width = bias.shape[-1]

    def at_x(d):
        return {"x": lax.rem(x + d, NX)}

    def at_z(d):
        return {"z": lax.rem(z + d + NZ, NZ)}

    sibling = {"core": other}

    barrier = pltpu.get_barrier_semaphore()
    near = [sibling, at_x(1), at_x(2), at_x(3)]
    near += [at_z(d) for d in (1, -1, 2, -2, 3, -3, 4, -4)]
    for peer in near:
        pl.semaphore_signal(barrier, inc=1, device_id=peer, device_id_type=pl.DeviceIdType.MESH)

    def greet(peers):
        for peer in peers:
            pl.semaphore_signal(
                barrier, inc=1, device_id=peer, device_id_type=pl.DeviceIdType.MESH)

    @pl.when(y > 0)
    def _():
        greet([{"y": y - 1}] + [{"y": y - 1, **at_x(d)} for d in (1, 2, 3)])

    @pl.when(y < NY - 1)
    def _():
        greet([{"y": y + 1}] + [{"y": y + 1, **at_z(d)} for d in (1, -1, 2, -2)])

    @pl.when(y == 0)
    def _():
        QB[...] = jnp.zeros_like(QB)

    @pl.when(y == NY - 1)
    def _():
        QN[...] = jnp.zeros_like(QN)

    mine = resid.at[y, :, pl.ds(pl.multiple_of(h * half, 128), half)]
    keep = pltpu.make_async_copy(mine, X.at[r, x, a], loc.at[0])
    keep.start()
    enc_own = pltpu.make_async_copy(
        enc.at[0, pl.ds(pl.multiple_of(h * half, 128), half), :],
        WE.at[:, pl.ds(pl.multiple_of(h * width, 128), width)], loc.at[1])
    enc_own.start()
    bias_own = pltpu.make_async_copy(bias, BI.at[h], loc.at[2])
    bias_own.start()
    tgt = pltpu.make_async_copy(
        target.at[pl.ds(y, 2), :, pl.ds(pl.multiple_of(h * half, 128), half)], TG, loc.at[3])
    tgt.start()
    dec_in = pltpu.make_async_copy(dec.at[0], DW, loc.at[4])
    dec_in.start()

    fire = pltpu.make_async_copy(blocks, BK, loc.at[7])
    fire.start()
    extra = jnp.where(y < NY - 1, 4, 0) + jnp.where(y > 0, 5, 0)
    pl.semaphore_wait(barrier, len(near) + extra)

    count = [0]
    started = []

    def made(src, dst, peer):
        k = count[0]
        count[0] += 1
        return pltpu.make_async_remote_copy(
            src_ref=src, dst_ref=dst, send_sem=ssem.at[k], recv_sem=rsem.at[k],
            device_id=peer, device_id_type=pl.DeviceIdType.MESH)

    def send(src, dst, peer):
        copy = made(src, dst, peer)
        copy.start()
        started.append(copy)
        return copy

    def slot(d):
        zz = lax.rem(z + d + NZ, NZ)
        return lax.rem(zz, 4), lax.div(zz, 4)

    def gathered(buf, src):
        own = buf.at[r, x, a]
        out = {d: send(src, own, at_z(d)) for d in (4, -4, 3, -3, 2, -2, 1, -1)}
        across = [send(src, own, at_x(d)) for d in (2, 1, 3)]

        def passed(d):
            rr, aa = slot(-d)
            got = buf.at[rr, x, aa]
            return got, [send(got, got, at_x(dx)) for dx in (2, 1, 3)]

        for d in (1, -1, 2, -2, 3, -3):
            out[d].wait_recv()
            across += passed(d)[1]
        far = {}
        for d, steps in ((4, (4, 3, 2, 1)), (-4, (-3, -2, -1))):
            out[d].wait_recv()
            rr, aa = slot(-d)
            got = buf.at[rr, x, aa]
            for k in steps:
                far[k + d] = send(got, got, at_z(k))
        for d in (4, -4):
            across += passed(d)[1]
        for d in (5, -5, 6, -6, 7, -7, 8):
            far[d].wait_recv()
            across += passed(d)[1]
        return across

    def gathered_even(buf):
        own = buf.at[r, x, a]
        out = {d: send(own, own, at_z(d)) for d in (4, -4, 3, -3, 2, -2, 1, -1)}
        sides = {}
        rest = [out[1], out[-1]]

        def to_sides(d):
            rr, aa = slot(-d)
            got = buf.at[rr, x, aa]
            sides[d] = [send(got, got, at_x(dx)) for dx in (2, 1, 3)]

        def to_next(d, ways):
            rr, aa = slot(-d)
            copies = []
            for dx, copy in zip((2, 1, 3), sides[d]):
                copy.wait_recv()
                got = buf.at[rr, lax.rem(x + NX - dx, NX), aa]
                copies += [send(got, got, at_z(way)) for way in ways]
            return copies

        to_sides(0)
        for d in (2, -2):
            out[d].wait_recv()
            to_sides(d)
        for d in (3, -3):
            out[d].wait_recv()
            to_sides(d)
        far = {}
        for d, steps in ((4, (4, 3, 2, 1)), (-4, (-3, -2, -1))):
            out[d].wait_recv()
            rr, aa = slot(-d)
            got = buf.at[rr, x, aa]
            for k in steps:
                far[k + d] = send(got, got, at_z(k))
        for d in (4, -4):
            to_sides(d)
        rest += to_next(0, (1, -1))
        for d in (6, -6, 7, -7, 8):
            far[d].wait_recv()
            to_sides(d)
        for d in (4, -4):
            rest += to_next(d, (1,) if d > 0 else (-1,))
        rest += [far[5], far[-5]]
        for d in (2, -2, 3, -3, 6, -6, 7, -7, 8):
            rest += sides[d]
        return rest

    enc_far = send(
        enc.at[0, pl.ds(pl.multiple_of(other * half, 128), half), :],
        WE.at[:, pl.ds(pl.multiple_of(h * width, 128), width)], sibling)
    bias_far = send(bias, BI.at[h], sibling)
    across = gathered(X, mine)

    fire.wait()
    row = BK[y]
    column = x * NZ + z
    hits = [
        jnp.max((row == g * NX * NZ + column).astype(F32), axis=1, keepdims=True)
        for g in range(2)
    ]
    lanes = lax.broadcasted_iota(jnp.int32, (1, 2 * width), 1)
    gates = jnp.where(lanes < width, hits[0], hits[1])
    gate_own = jnp.where(h == 0, hits[0], hits[1])

    bias_far.wait_recv()
    bias_own.wait()
    enc_far.wait_recv()
    enc_own.wait()
    keep.wait()
    for copy in across:
        copy.wait_recv()
    for rr in range(4):
        XO[pl.ds(rr * 32, 32), :] = X[rr].reshape(32, half)
    PP[...] = jnp.dot(XO[...], WE[...], preferred_element_type=F32)
    part = send(PP, PR, sibling)
    part.wait_recv()
    biases = jnp.concatenate([BI[0], BI[1]], axis=1)
    acts = ((PP[...] + PR[...] + biases) * gates).astype(BF16)

    dec_in.wait()
    step = 256
    n2 = half // 2
    lo, hi = pl.ds(0, n2), pl.ds(n2, n2)
    r1, r3, r2 = lax.rem(r + 1, 4), lax.rem(r + 3, 4), lax.rem(r + 2, 4)
    classes = ((2, r2), (1, r1), (3, r3), (0, r))
    in1, in0 = {}, {}
    for t, S in ((1, S1), (0, S0)):
        for n in range(0, half, step):
            w = DW[t, :, :, n:n + step].reshape(2 * width, step)
            p = jnp.dot(acts, w, preferred_element_type=F32)
            S[:, :, :, n:n + step] = p.reshape(4, NX, 8, step).astype(BF16)
        if t == 1:
            for d in (2, 1, 3, 0):
                xx = lax.rem(x + d, NX)
                in1[d] = [
                    send(S1.at[r2, xx, :, lo], R1.at[2, xx, :, lo], at_z(2)),
                    send(S1.at[r2, xx, :, hi], R1.at[2, xx, :, hi], at_z(-2)),
                    send(S1.at[r1, xx], R1.at[0, xx], at_z(1)),
                    send(S1.at[r3, xx], R1.at[1, xx], at_z(-1)),
                ]
        else:
            for d, rr in classes:
                in0[d] = [
                    send(S0.at[rr, lax.rem(x + dx, NX)], R0.at[i, rr], at_x(dx))
                    for i, dx in enumerate((2, 1, 3))
                ]
    for n in range(0, half, step):
        x_out[h, n:n + step, :] = XO[:, n:n + step].T
    rows_far = send(x_out.at[h], XS_T, sibling)

    def summed1(xx):
        return (S1[r, xx].astype(F32) + R1[0, xx].astype(F32)) + (
            R1[1, xx].astype(F32) + R1[2, xx].astype(F32))

    def summed0(rr):
        return (S0[rr, x].astype(F32) + R0[0, rr].astype(F32)) + (
            R0[1, rr].astype(F32) + R0[2, rr].astype(F32))

    def landed(copies):
        for copy in copies:
            copy.wait_recv()

    after, above, below = [], [], []
    up_y = {"y": lax.rem(y + 1, NY)}
    down_y = {"y": lax.rem(y + NY - 1, NY)}

    def start_above(*copies):
        above.extend(copies)

        @pl.when(y < NY - 1)
        def _():
            for copy in copies:
                copy.start()

    def start_below(*copies):
        below.extend(copies)

        @pl.when(y > 0)
        def _():
            for copy in copies:
                copy.start()

    for i, (d, rr) in enumerate(classes[:3]):
        landed(in1[d])
        B1[i] = summed1(lax.rem(x + d, NX)).astype(BF16)
        start_above(made(B1.at[i], QB.at[i], {**up_y, **at_x(d)}))
        after.append(send(B1.at[i], Q1.at[i], at_x(d)))
        landed(in0[d])
        B0[i] = summed0(rr).astype(BF16)
        if d == 2:
            parts = ((lo, at_z(2)), (hi, at_z(-2)))
            start_below(*[
                made(B0.at[i, :, cols], QN.at[i, :, cols], {**down_y, **to})
                for cols, to in parts
            ])
            after += [send(B0.at[i, :, cols], Q0.at[i, :, cols], to) for cols, to in parts]
        else:
            to = at_z(1 if d == 1 else -1)
            start_below(made(B0.at[i], QN.at[i], {**down_y, **to}))
            after.append(send(B0.at[i], Q0.at[i], to))
    landed(in1[0])
    own1 = summed1(x)
    B1[3] = own1.astype(BF16)
    start_above(made(B1.at[3], QB.at[3], up_y))
    landed(in0[0])
    own0 = summed0(r)
    B0[3] = own0.astype(BF16)
    start_below(made(B0.at[3], QN.at[3], down_y))
    landed(after)

    @pl.when(y > 0)
    def _():
        landed(above)

    @pl.when(y < NY - 1)
    def _():
        landed(below)

    for t, own, Q, QY in ((0, own0, Q0, QB), (1, own1, Q1, QN)):
        total = (own + Q[0].astype(F32)) + (Q[1].astype(F32) + Q[2].astype(F32))
        total = total + (
            (QY[0].astype(F32) + QY[1].astype(F32)) + (QY[2].astype(F32) + QY[3].astype(F32)))
        for aa in range(NA):
            two = total[2 * aa:2 * aa + 2, :]
            S2F[aa, t] = two
            S2[aa, t] = two.astype(BF16)
    last = [
        send(S2.at[lax.rem(a + d, NA)], R2.at[i], at_z(4 * d if d < 3 else -4))
        for i, d in enumerate((2, 1, 3))
    ]
    rows_far.wait_recv()
    out_b = pltpu.make_async_copy(XS_T, x_out.at[other], loc.at[5])
    out_b.start()
    for copy in last:
        copy.wait_recv()
    sums = S2F[a] + R2[0].astype(F32) + R2[1].astype(F32) + R2[2].astype(F32)

    tgt.wait()
    err_own = (sums[0] - TG[0].astype(F32)).astype(BF16)
    err_next = (sums[1] - TG[1].astype(F32)).astype(BF16)
    err_out[0] = err_own
    E[r, x, a, 0] = err_own
    E[r, x, a, 1] = err_next

    for copy in gathered_even(E):
        copy.wait_recv()
    for t in range(2):
        for rr in range(4):
            EM[t, pl.ds(rr * 32, 32), :] = E[rr, :, :, t].reshape(32, half)

    def latent_grad(g):
        terms = [
            lax.dot_general(
                EM[t], DW[t, g], (((1,), (1,)), ((), ())), preferred_element_type=F32)
            for t in range(2)
        ]
        return terms[0] + terms[1]

    GP[...] = latent_grad(other)
    back = send(GP, GR, sibling)
    grad_own = latent_grad(h)
    back.wait_recv()
    grad_pre = (grad_own + GR[...]) * gate_own
    bias_out[...] = jnp.sum(grad_pre, axis=0, keepdims=True)
    low_out[...] = grad_pre.astype(BF16)
    for copy in started:
        copy.wait_send()

    @pl.when(y < NY - 1)
    def _():
        for copy in above:
            copy.wait_send()

    @pl.when(y > 0)
    def _():
        for copy in below:
            copy.wait_send()

    out_b.wait()


def on_device(resid, target, enc, bias, dec, blocks):
    half = dec.shape[-1]
    width = enc.shape[-1]
    rows = 128
    hbm = pl.BlockSpec(memory_space=pltpu.HBM)
    vmem = pl.BlockSpec(memory_space=pltpu.VMEM)
    V = pltpu.VMEM
    resid, target, enc, bias, dec, blocks = (
        pltpu.with_memory_space_constraint(v, pltpu.HBM)
        for v in (resid, target, enc, bias, dec, blocks))
    x_all, low, bias_grad, errors = pl.pallas_call(
        body,
        out_shape=(
            jax.ShapeDtypeStruct((2, half, rows), BF16),
            jax.ShapeDtypeStruct((rows, width), BF16),
            jax.ShapeDtypeStruct((1, width), F32),
            jax.ShapeDtypeStruct((1, 2, half), BF16),
        ),
        in_specs=[hbm] * 6,
        out_specs=(vmem,) * 4,
        scratch_shapes=[
            V((4, NX, NA, 2, half), BF16),
            V((rows, half), BF16),
            V((half, rows), BF16),
            V((half, 2 * width), BF16),
            V((2, 1, width), F32),
            V((2, 2, width, half), BF16),
            V((2, 2, half), BF16),
            V((rows, 2 * width), F32),
            V((rows, 2 * width), F32),
            V((4, NX, 8, half), BF16),
            V((4, NX, 8, half), BF16),
            V((3, 4, 8, half), BF16),
            V((3, NX, 8, half), BF16),
            V((4, 8, half), BF16),
            V((4, 8, half), BF16),
            V((3, 8, half), BF16),
            V((3, 8, half), BF16),
            V((NA, 2, 2, half), BF16),
            V((NA, 2, 2, half), F32),
            V((3, 2, 2, half), BF16),
            V((4, 8, half), BF16),
            V((4, 8, half), BF16),
            V((4, NX, NA, 2, 2, half), BF16),
            V((2, rows, half), BF16),
            V((rows, width), F32),
            V((rows, width), F32),
            V(blocks.shape, jnp.int32),
            pltpu.SemaphoreType.DMA((8,)),
            pltpu.SemaphoreType.DMA((SENDS,)),
            pltpu.SemaphoreType.DMA((SENDS,)),
        ],
        compiler_params=pltpu.CompilerParams(
            collective_id=0, has_side_effects=True, vmem_limit_bytes=53700 << 10),
        name="step",
    )(resid, target, enc, bias, dec, blocks)
    tall = 2 * half // PARTS
    grad, bias_grad, errors = pl.pallas_call(
        weight_gradient,
        out_shape=(
            jax.ShapeDtypeStruct((1, 2 * half, width), BF16),
            jax.ShapeDtypeStruct((1, width), F32),
            jax.ShapeDtypeStruct((1, 2, half), BF16),
        ),
        in_specs=[vmem] * 4,
        out_specs=(hbm, vmem, vmem),
        scratch_shapes=[V((PARTS, tall, width), BF16), pltpu.SemaphoreType.DMA((PARTS,))],
        compiler_params=pltpu.CompilerParams(vmem_limit_bytes=8 << 20),
        name="weights",
    )(x_all.reshape(2 * half, rows), low, bias_grad, errors)
    return errors, grad, bias_grad


def weight_gradient(xt, low, bias_in, err_in, grad, bias_out, err_out, held, sems):
    tall = held.shape[1]
    copies = []
    for i in range(PARTS):
        part = jnp.dot(xt[i * tall:(i + 1) * tall, :], low[...], preferred_element_type=F32)
        held[i] = part.astype(BF16)
        copies.append(pltpu.make_async_copy(
            held.at[i], grad.at[0, pl.ds(i * tall, tall), :], sems.at[i]))
        copies[-1].start()
    bias_out[...] = bias_in[...]
    err_out[...] = err_in[...]
    for copy in copies:
        copy.wait()


def solution(mesh):
    fine = Mesh(mesh.devices.reshape(NY, 2, NX, NZ), ("y", "core", "x", "z"))
    layer, latent = ("y", "core"), ("x", "z")
    return jax.shard_map(
        on_device,
        mesh=fine,
        in_specs=(
            P(None, latent, None), P(None, latent, None), P(layer, None, latent),
            P(layer, latent), P(layer, None, None, latent, None), P(),
        ),
        out_specs=(P(layer, latent, None), P(layer, None, latent), P(layer, latent)),
        check_vma=False,
    )
```

```python
import functools

import jax
import jax.numpy as jnp
from jax import lax
from jax.experimental import pallas as pl
from jax.experimental.pallas import tpu as pltpu
from jax.sharding import Mesh
from jax.sharding import PartitionSpec as P

NY, NX, NZ = 4, 4, 16
NA = 4
F32, BF16 = jnp.float32, jnp.bfloat16
SENDS = 216
PARTS = 7


def body(
    resid, target, enc, bias, dec, blocks,
    x_out, low_out, bias_out, err_out,
    X, XO, XS_T, WE, BI, DW, TG, PP, PR, S0, S1, R0, R1, B0, B1, Q0, Q1,
    S2, S2F, R2, QN, QB, E, EM, GP, GR, BK, loc, ssem, rsem,
):
    y, h = lax.axis_index("y"), lax.axis_index("core")
    x, z = lax.axis_index("x"), lax.axis_index("z")
    other = 1 - h
    r, a = lax.rem(z, 4), lax.div(z, 4)
    half = XO.shape[-1]
    width = bias.shape[-1]

    def at_x(d):
        return {"x": lax.rem(x + d, NX)}

    def at_z(d):
        return {"z": lax.rem(z + d + NZ, NZ)}

    sibling = {"core": other}

    barrier = pltpu.get_barrier_semaphore()
    near = [sibling, at_x(1), at_x(2), at_x(3)]
    near += [at_z(d) for d in (1, -1, 2, -2, 3, -3, 4, -4)]
    for peer in near:
        pl.semaphore_signal(barrier, inc=1, device_id=peer, device_id_type=pl.DeviceIdType.MESH)

    def greet(peers):
        for peer in peers:
            pl.semaphore_signal(
                barrier, inc=1, device_id=peer, device_id_type=pl.DeviceIdType.MESH)

    @pl.when(y > 0)
    def _():
        greet([{"y": y - 1}] + [{"y": y - 1, **at_x(d)} for d in (1, 2, 3)])

    @pl.when(y < NY - 1)
    def _():
        greet([{"y": y + 1}] + [{"y": y + 1, **at_z(d)} for d in (1, -1, 2, -2)])

    @pl.when(y == 0)
    def _():
        QB[...] = jnp.zeros_like(QB)

    @pl.when(y == NY - 1)
    def _():
        QN[...] = jnp.zeros_like(QN)

    mine = resid.at[y, :, pl.ds(pl.multiple_of(h * half, 128), half)]
    keep = pltpu.make_async_copy(mine, X.at[r, x, a], loc.at[0])
    keep.start()
    enc_own = pltpu.make_async_copy(
        enc.at[0, pl.ds(pl.multiple_of(h * half, 128), half), :],
        WE.at[:, pl.ds(pl.multiple_of(h * width, 128), width)], loc.at[1])
    enc_own.start()
    bias_own = pltpu.make_async_copy(bias, BI.at[h], loc.at[2])
    bias_own.start()
    tgt = pltpu.make_async_copy(
        target.at[pl.ds(y, 2), :, pl.ds(pl.multiple_of(h * half, 128), half)], TG, loc.at[3])
    tgt.start()
    dec_in = pltpu.make_async_copy(dec.at[0], DW, loc.at[4])
    dec_in.start()

    fire = pltpu.make_async_copy(blocks, BK, loc.at[7])
    fire.start()
    extra = jnp.where(y < NY - 1, 4, 0) + jnp.where(y > 0, 5, 0)
    pl.semaphore_wait(barrier, len(near) + extra)

    count = [0]
    started = []

    def made(src, dst, peer):
        k = count[0]
        count[0] += 1
        return pltpu.make_async_remote_copy(
            src_ref=src, dst_ref=dst, send_sem=ssem.at[k], recv_sem=rsem.at[k],
            device_id=peer, device_id_type=pl.DeviceIdType.MESH)

    def send(src, dst, peer):
        copy = made(src, dst, peer)
        copy.start()
        started.append(copy)
        return copy

    def slot(d):
        zz = lax.rem(z + d + NZ, NZ)
        return lax.rem(zz, 4), lax.div(zz, 4)

    def gathered(buf, src):
        own = buf.at[r, x, a]
        out = {d: send(src, own, at_z(d)) for d in (4, -4, 3, -3, 2, -2, 1, -1)}
        sides = {}
        rest = [out[1], out[-1]]

        def to_sides(d):
            rr, aa = slot(-d)
            got = buf.at[rr, x, aa]
            sides[d] = [send(got, got, at_x(dx)) for dx in (2, 1, 3)]

        def to_next(d, ways):
            rr, aa = slot(-d)
            copies = []
            for dx, copy in zip((2, 1, 3), sides[d]):
                copy.wait_recv()
                got = buf.at[rr, lax.rem(x + NX - dx, NX), aa]
                copies += [send(got, got, at_z(way)) for way in ways]
            return copies

        sides[0] = [send(src, own, at_x(dx)) for dx in (2, 1, 3)]
        for d in (2, -2):
            out[d].wait_recv()
            to_sides(d)
        for d in (3, -3):
            out[d].wait_recv()
            to_sides(d)
        far = {}
        for d, steps in ((4, (4, 3, 2, 1)), (-4, (-3, -2, -1))):
            out[d].wait_recv()
            rr, aa = slot(-d)
            got = buf.at[rr, x, aa]
            for k in steps:
                far[k + d] = send(got, got, at_z(k))
        for d in (4, -4):
            to_sides(d)
        rest += to_next(0, (1, -1))
        for d in (6, -6, 7, -7, 8):
            far[d].wait_recv()
            to_sides(d)
        for d in (4, -4):
            rest += to_next(d, (1,) if d > 0 else (-1,))
        rest += [far[5], far[-5]]
        for d in (2, -2, 3, -3, 6, -6, 7, -7, 8):
            rest += sides[d]
        return rest

    enc_far = send(
        enc.at[0, pl.ds(pl.multiple_of(other * half, 128), half), :],
        WE.at[:, pl.ds(pl.multiple_of(h * width, 128), width)], sibling)
    bias_far = send(bias, BI.at[h], sibling)
    across = gathered(X, mine)

    fire.wait()
    row = BK[y]
    column = x * NZ + z
    hits = [
        jnp.max((row == g * NX * NZ + column).astype(F32), axis=1, keepdims=True)
        for g in range(2)
    ]
    lanes = lax.broadcasted_iota(jnp.int32, (1, 2 * width), 1)
    gates = jnp.where(lanes < width, hits[0], hits[1])
    gate_own = jnp.where(h == 0, hits[0], hits[1])

    bias_far.wait_recv()
    bias_own.wait()
    enc_far.wait_recv()
    enc_own.wait()
    keep.wait()
    for copy in across:
        copy.wait_recv()
    for rr in range(4):
        XO[pl.ds(rr * 32, 32), :] = X[rr].reshape(32, half)
    PP[...] = jnp.dot(XO[...], WE[...], preferred_element_type=F32)
    part = send(PP, PR, sibling)
    part.wait_recv()
    biases = jnp.concatenate([BI[0], BI[1]], axis=1)
    acts = ((PP[...] + PR[...] + biases) * gates).astype(BF16)

    dec_in.wait()
    step = 256
    n2 = half // 2
    lo, hi = pl.ds(0, n2), pl.ds(n2, n2)
    r1, r3, r2 = lax.rem(r + 1, 4), lax.rem(r + 3, 4), lax.rem(r + 2, 4)
    classes = ((2, r2), (1, r1), (3, r3), (0, r))
    in1, in0 = {}, {}
    for t, S in ((1, S1), (0, S0)):
        for n in range(0, half, step):
            w = DW[t, :, :, n:n + step].reshape(2 * width, step)
            p = jnp.dot(acts, w, preferred_element_type=F32)
            S[:, :, :, n:n + step] = p.reshape(4, NX, 8, step).astype(BF16)
        if t == 1:
            for d in (2, 1, 3, 0):
                xx = lax.rem(x + d, NX)
                in1[d] = [
                    send(S1.at[r2, xx, :, lo], R1.at[2, xx, :, lo], at_z(2)),
                    send(S1.at[r2, xx, :, hi], R1.at[2, xx, :, hi], at_z(-2)),
                    send(S1.at[r1, xx], R1.at[0, xx], at_z(1)),
                    send(S1.at[r3, xx], R1.at[1, xx], at_z(-1)),
                ]
        else:
            for d, rr in classes:
                in0[d] = [
                    send(S0.at[rr, lax.rem(x + dx, NX)], R0.at[i, rr], at_x(dx))
                    for i, dx in enumerate((2, 1, 3))
                ]
    for n in range(0, half, step):
        x_out[h, n:n + step, :] = XO[:, n:n + step].T
    rows_far = send(x_out.at[h], XS_T, sibling)

    def summed1(xx):
        return (S1[r, xx].astype(F32) + R1[0, xx].astype(F32)) + (
            R1[1, xx].astype(F32) + R1[2, xx].astype(F32))

    def summed0(rr):
        return (S0[rr, x].astype(F32) + R0[0, rr].astype(F32)) + (
            R0[1, rr].astype(F32) + R0[2, rr].astype(F32))

    def landed(copies):
        for copy in copies:
            copy.wait_recv()

    after, above, below = [], [], []
    up_y = {"y": lax.rem(y + 1, NY)}
    down_y = {"y": lax.rem(y + NY - 1, NY)}

    def start_above(*copies):
        above.extend(copies)

        @pl.when(y < NY - 1)
        def _():
            for copy in copies:
                copy.start()

    def start_below(*copies):
        below.extend(copies)

        @pl.when(y > 0)
        def _():
            for copy in copies:
                copy.start()

    for i, (d, rr) in enumerate(classes[:3]):
        landed(in1[d])
        B1[i] = summed1(lax.rem(x + d, NX)).astype(BF16)
        start_above(made(B1.at[i], QB.at[i], {**up_y, **at_x(d)}))
        after.append(send(B1.at[i], Q1.at[i], at_x(d)))
        landed(in0[d])
        B0[i] = summed0(rr).astype(BF16)
        if d == 2:
            parts = ((lo, at_z(2)), (hi, at_z(-2)))
            start_below(*[
                made(B0.at[i, :, cols], QN.at[i, :, cols], {**down_y, **to})
                for cols, to in parts
            ])
            after += [send(B0.at[i, :, cols], Q0.at[i, :, cols], to) for cols, to in parts]
        else:
            to = at_z(1 if d == 1 else -1)
            start_below(made(B0.at[i], QN.at[i], {**down_y, **to}))
            after.append(send(B0.at[i], Q0.at[i], to))
    landed(in1[0])
    own1 = summed1(x)
    B1[3] = own1.astype(BF16)
    start_above(made(B1.at[3], QB.at[3], up_y))
    landed(in0[0])
    own0 = summed0(r)
    B0[3] = own0.astype(BF16)
    start_below(made(B0.at[3], QN.at[3], down_y))
    landed(after)

    @pl.when(y > 0)
    def _():
        landed(above)

    @pl.when(y < NY - 1)
    def _():
        landed(below)

    for t, own, Q, QY in ((0, own0, Q0, QB), (1, own1, Q1, QN)):
        total = (own + Q[0].astype(F32)) + (Q[1].astype(F32) + Q[2].astype(F32))
        total = total + (
            (QY[0].astype(F32) + QY[1].astype(F32)) + (QY[2].astype(F32) + QY[3].astype(F32)))
        for aa in range(NA):
            two = total[2 * aa:2 * aa + 2, :]
            S2F[aa, t] = two
            S2[aa, t] = two.astype(BF16)
    last = [
        send(S2.at[lax.rem(a + d, NA)], R2.at[i], at_z(4 * d if d < 3 else -4))
        for i, d in enumerate((2, 1, 3))
    ]
    rows_far.wait_recv()
    out_b = pltpu.make_async_copy(XS_T, x_out.at[other], loc.at[5])
    out_b.start()
    for copy in last:
        copy.wait_recv()
    sums = S2F[a] + R2[0].astype(F32) + R2[1].astype(F32) + R2[2].astype(F32)

    tgt.wait()
    err_own = (sums[0] - TG[0].astype(F32)).astype(BF16)
    err_next = (sums[1] - TG[1].astype(F32)).astype(BF16)
    err_out[0] = err_own
    E[r, x, a, 0] = err_own
    E[r, x, a, 1] = err_next

    for copy in gathered(E, E.at[r, x, a]):
        copy.wait_recv()
    for t in range(2):
        for rr in range(4):
            EM[t, pl.ds(rr * 32, 32), :] = E[rr, :, :, t].reshape(32, half)

    def latent_grad(g):
        terms = [
            lax.dot_general(
                EM[t], DW[t, g], (((1,), (1,)), ((), ())), preferred_element_type=F32)
            for t in range(2)
        ]
        return terms[0] + terms[1]

    GP[...] = latent_grad(other)
    back = send(GP, GR, sibling)
    grad_own = latent_grad(h)
    back.wait_recv()
    grad_pre = (grad_own + GR[...]) * gate_own
    bias_out[...] = jnp.sum(grad_pre, axis=0, keepdims=True)
    low_out[...] = grad_pre.astype(BF16)
    for copy in started:
        copy.wait_send()

    @pl.when(y < NY - 1)
    def _():
        for copy in above:
            copy.wait_send()

    @pl.when(y > 0)
    def _():
        for copy in below:
            copy.wait_send()

    out_b.wait()


def on_device(resid, target, enc, bias, dec, blocks):
    half = dec.shape[-1]
    width = enc.shape[-1]
    rows = 128
    hbm = pl.BlockSpec(memory_space=pltpu.HBM)
    vmem = pl.BlockSpec(memory_space=pltpu.VMEM)
    V = pltpu.VMEM
    resid, target, enc, bias, dec, blocks = (
        pltpu.with_memory_space_constraint(v, pltpu.HBM)
        for v in (resid, target, enc, bias, dec, blocks))
    x_all, low, bias_grad, errors = pl.pallas_call(
        body,
        out_shape=(
            jax.ShapeDtypeStruct((2, half, rows), BF16),
            jax.ShapeDtypeStruct((rows, width), BF16),
            jax.ShapeDtypeStruct((1, width), F32),
            jax.ShapeDtypeStruct((1, 2, half), BF16),
        ),
        in_specs=[hbm] * 6,
        out_specs=(vmem,) * 4,
        scratch_shapes=[
            V((4, NX, NA, 2, half), BF16),
            V((rows, half), BF16),
            V((half, rows), BF16),
            V((half, 2 * width), BF16),
            V((2, 1, width), F32),
            V((2, 2, width, half), BF16),
            V((2, 2, half), BF16),
            V((rows, 2 * width), F32),
            V((rows, 2 * width), F32),
            V((4, NX, 8, half), BF16),
            V((4, NX, 8, half), BF16),
            V((3, 4, 8, half), BF16),
            V((3, NX, 8, half), BF16),
            V((4, 8, half), BF16),
            V((4, 8, half), BF16),
            V((3, 8, half), BF16),
            V((3, 8, half), BF16),
            V((NA, 2, 2, half), BF16),
            V((NA, 2, 2, half), F32),
            V((3, 2, 2, half), BF16),
            V((4, 8, half), BF16),
            V((4, 8, half), BF16),
            V((4, NX, NA, 2, 2, half), BF16),
            V((2, rows, half), BF16),
            V((rows, width), F32),
            V((rows, width), F32),
            V(blocks.shape, jnp.int32),
            pltpu.SemaphoreType.DMA((8,)),
            pltpu.SemaphoreType.DMA((SENDS,)),
            pltpu.SemaphoreType.DMA((SENDS,)),
        ],
        compiler_params=pltpu.CompilerParams(
            collective_id=0, has_side_effects=True, vmem_limit_bytes=53700 << 10),
        name="step",
    )(resid, target, enc, bias, dec, blocks)
    tall = 2 * half // PARTS
    grad, bias_grad, errors = pl.pallas_call(
        weight_gradient,
        out_shape=(
            jax.ShapeDtypeStruct((1, 2 * half, width), BF16),
            jax.ShapeDtypeStruct((1, width), F32),
            jax.ShapeDtypeStruct((1, 2, half), BF16),
        ),
        in_specs=[vmem] * 4,
        out_specs=(hbm, vmem, vmem),
        scratch_shapes=[V((PARTS, tall, width), BF16), pltpu.SemaphoreType.DMA((PARTS,))],
        compiler_params=pltpu.CompilerParams(vmem_limit_bytes=8 << 20),
        name="weights",
    )(x_all.reshape(2 * half, rows), low, bias_grad, errors)
    return errors, grad, bias_grad


def weight_gradient(xt, low, bias_in, err_in, grad, bias_out, err_out, held, sems):
    tall = held.shape[1]
    copies = []
    for i in range(PARTS):
        part = jnp.dot(xt[i * tall:(i + 1) * tall, :], low[...], preferred_element_type=F32)
        held[i] = part.astype(BF16)
        copies.append(pltpu.make_async_copy(
            held.at[i], grad.at[0, pl.ds(i * tall, tall), :], sems.at[i]))
        copies[-1].start()
    bias_out[...] = bias_in[...]
    err_out[...] = err_in[...]
    for copy in copies:
        copy.wait()


def solution(mesh):
    fine = Mesh(mesh.devices.reshape(NY, 2, NX, NZ), ("y", "core", "x", "z"))
    layer, latent = ("y", "core"), ("x", "z")
    return jax.shard_map(
        on_device,
        mesh=fine,
        in_specs=(
            P(None, latent, None), P(None, latent, None), P(layer, None, latent),
            P(layer, latent), P(layer, None, None, latent, None), P(),
        ),
        out_specs=(P(layer, latent, None), P(layer, None, latent), P(layer, latent)),
        check_vma=False,
    )
```
